256 devices in a mesh: dp: 16 (over z, core), expert: 16 (over x, y).
Axes of the slice: x: 4, y: 4, z: 8, core: 2. Of those that a mesh axis runs over, the one named last changes fastest.
Arguments:
- tokens: bfloat16 [32768, 2048], P(('dp', 'expert')), may hold values from -6 to 6
- expert_ids: int32 [32768, 4], P(('dp', 'expert')), may hold values from 0 to 31, as said below
- gate_weights: float32 [32768, 4], P(('dp', 'expert')), may hold values from 0.1 to 0.6
- hot_ids: int32 [2], replicated, may hold values from 0 to 31, as said below
- w_gate: bfloat16 [32, 2048, 768], P('expert', 'dp'), may hold values from -0.125 to 0.125
- w_up: bfloat16 [32, 2048, 768], P('expert', 'dp'), may hold values from -0.125 to 0.125
- w_down: bfloat16 [32, 768, 2048], P('expert', None, 'dp'), may hold values from -0.21875 to 0.21875
Outputs:
- moe_out: bfloat16 [32768, 2048], P(('dp', 'expert'))
The draws below stay inside these ranges and needn't reach their ends.
Inputs may be any that keep to these rules, and one draw needn't show every extreme that they name: `expert_ids`: tokens are in aligned blocks of 128 rows, one block a device. Column 0 of each row names an expert of hot_ids, each listed expert exactly 64 times in every block. Columns 1 to 3 name experts outside hot_ids, all different within a row; each such expert appears at most 24 times in a block, and one of them exactly 24 times in every block. `hot_ids`: the listed experts are all different, and one of them is expert 32 - 1.
All inputs are finite; a program needn't handle non-finite values.
Results may differ from the reference program's by a relative error of at most 0.0057.
Values may be sent and summed in bfloat16 or wider, within the bound.
A program may use at most 384 MiB of HBM per device.

```python
import jax
import jax.numpy as jnp
from jax import lax

D = 2048
FF = 768
TOP = 4
HOT = 2
TOK_DEV = 128
EXPERTS = 32
TOKENS = 32768
CAP = 24
HCAP = 64


def route_tables(key):
    blocks = TOKENS // TOK_DEV
    cold_count = EXPERTS - HOT
    grid_count = cold_count * CAP
    pair_count = TOK_DEV * (TOP - 1)
    others = jax.random.permutation(jax.random.fold_in(key, 11), EXPERTS - 1).astype(jnp.int32)
    last_one = jnp.full((1,), EXPERTS - 1, jnp.int32)
    hot_drawn = jnp.concatenate([last_one, others[:HOT - 1]], axis=0)
    hot_order = jax.random.permutation(jax.random.fold_in(key, 17), HOT).astype(jnp.int32)
    hot_list = hot_drawn[hot_order]
    cold_list = others[HOT - 1:]

    def one_block(block_key):
        key_first = jax.random.fold_in(block_key, 1)
        key_grid = jax.random.fold_in(block_key, 2)
        key_second = jax.random.fold_in(block_key, 3)
        token_perm = jax.random.permutation(key_first, TOK_DEV).astype(jnp.int32)
        hot_column = jnp.zeros((TOK_DEV,), jnp.int32).at[token_perm].set(hot_list[jnp.arange(TOK_DEV, dtype=jnp.int32) % HOT])
        positions = jnp.arange(grid_count, dtype=jnp.int32)
        scores = jax.random.permutation(key_grid, grid_count).astype(jnp.int32) + grid_count
        scores = jnp.where(positions < CAP, positions, scores)
        picked_slots = jnp.sort(jnp.argsort(scores)[:pair_count].astype(jnp.int32))
        chosen = cold_list[picked_slots // CAP].reshape(TOP - 1, TOK_DEV)
        second_perm = jax.random.permutation(key_second, TOK_DEV).astype(jnp.int32)
        cold_columns = jnp.zeros((TOK_DEV, TOP - 1), jnp.int32).at[second_perm].set(chosen.T)
        return jnp.concatenate([hot_column[:, None], cold_columns], axis=1)
    block_keys = jax.random.split(jax.random.fold_in(key, 13), blocks)
    route_ids = jax.vmap(one_block)(block_keys).reshape(TOKENS, TOP)
    return (route_ids, hot_list)


def draw_expert_ids(key, part):
    route_ids, hot_list = route_tables(jax.random.fold_in(key, 5))
    return route_ids


def draw_hot_ids(key, part):
    route_ids, hot_list = route_tables(jax.random.fold_in(key, 5))
    return hot_list


def shard_levels(own_key, dims, pieces, smallest, top_value):
    gain = 1.0
    for dim, blocks in pieces:
        heights = jax.random.uniform(jax.random.fold_in(jax.random.fold_in(own_key, 6), dim), (blocks,), jnp.float32, smallest / len(pieces), top_value / len(pieces))
        gain = gain * jnp.repeat(jnp.exp(heights), dims[dim] // blocks).reshape((-1,) + (1,) * (len(dims) - 1 - dim))
    return gain


def bell_draw(own_key, shape, deviation, reach, pieces=(), kind=jnp.bfloat16):
    level = shard_levels(own_key, shape, pieces, -0.22, 0.18) if pieces else 1.0
    result = jax.random.normal(own_key, shape, jnp.float32) * deviation * level
    return jnp.minimum(jnp.maximum(result, -reach), reach).astype(kind)


def setup_inputs(seed: int = 0) -> dict:
    splits = jax.random.split(jax.random.key(seed), 8)
    tokens = bell_draw(splits[0], (TOKENS, D), 1.0, 6.0, ((0, 256),))
    expert_ids = draw_expert_ids(jax.random.fold_in(splits[7], 71), 0)
    gate_weights = jnp.clip(0.1 + 0.5 * jax.random.uniform(splits[2], (TOKENS, TOP), jnp.float32) ** shard_levels(splits[2], (TOKENS, TOP), ((0, 256),), -0.2, 0.2), 0.1, 0.6)
    hot_ids = draw_hot_ids(jax.random.fold_in(splits[7], 71), 0)
    w_gate = bell_draw(splits[4], (EXPERTS, D, FF), D ** -0.5, 0.125, ((0, 16), (1, 16)))
    w_up = bell_draw(splits[5], (EXPERTS, D, FF), D ** -0.5, 0.125, ((0, 16), (1, 16)))
    w_down = bell_draw(splits[6], (EXPERTS, FF, D), FF ** -0.5, 0.21875, ((0, 16), (2, 16)))
    return dict(tokens=tokens, expert_ids=expert_ids, gate_weights=gate_weights, hot_ids=hot_ids, w_gate=w_gate, w_up=w_up, w_down=w_down)


def expert_apply(row_block, gate_weight, up_weight, down_weight):
    gate_sum = jnp.dot(row_block, gate_weight, preferred_element_type=jnp.float32)
    up_sum = jnp.dot(row_block, up_weight, preferred_element_type=jnp.float32)
    hidden = (jax.nn.silu(gate_sum) * up_sum).astype(jnp.bfloat16)
    return jnp.dot(hidden, down_weight, preferred_element_type=jnp.float32).astype(jnp.bfloat16)


def routed(token_blocks, route_ids, gate_table, expert, slot_cap, gate_weight, up_weight, down_weight):
    blocks, tok_dev, model_width = token_blocks.shape
    slot_count = route_ids.shape[2]
    pair_count = tok_dev * slot_count
    flat_ids = route_ids.reshape(blocks, pair_count)
    flat_gates = gate_table.reshape(blocks, pair_count)
    is_hit = flat_ids == expert
    rank_index = jnp.cumsum(is_hit.astype(jnp.int32), axis=1).astype(jnp.int32) - 1
    slot_where = jnp.where(is_hit, rank_index, slot_cap).astype(jnp.int32)
    pair_index = jnp.broadcast_to(jnp.arange(pair_count, dtype=jnp.int32)[None, :], (blocks, pair_count))
    block_rows = jnp.broadcast_to(jnp.arange(blocks, dtype=jnp.int32)[:, None], (blocks, pair_count))
    slot_table = jnp.full((blocks, slot_cap + 1), pair_count, jnp.int32)
    slot_table = slot_table.at[block_rows, slot_where].set(pair_index)[:, :slot_cap]
    token_index = (slot_table // slot_count).astype(jnp.int32)
    gates_padded = jnp.concatenate([flat_gates, jnp.zeros((blocks, 1), jnp.float32)], axis=1)
    weighting = jnp.take_along_axis(gates_padded, slot_table, axis=1)
    padded = jnp.concatenate([token_blocks, jnp.zeros((blocks, 1, model_width), jnp.bfloat16)], axis=1)
    block_index = jnp.arange(blocks, dtype=jnp.int32)[:, None]
    row_block = padded[block_index, token_index]
    expert_out = expert_apply(row_block.reshape(blocks * slot_cap, model_width), gate_weight, up_weight, down_weight)
    contribution = expert_out.reshape(blocks, slot_cap, model_width).astype(jnp.float32) * weighting[:, :, None]
    accum_sum = jnp.zeros((blocks, tok_dev + 1, model_width), jnp.float32)
    accum_sum = accum_sum.at[block_index, token_index].add(contribution)
    return accum_sum[:, :tok_dev]


def reference(tokens, expert_ids, gate_weights, hot_ids, w_gate, w_up, w_down):
    blocks = TOKENS // TOK_DEV
    token_blocks = tokens.reshape(blocks, TOK_DEV, D)
    route_ids = expert_ids.reshape(blocks, TOK_DEV, TOP)
    gate_table = gate_weights.reshape(blocks, TOK_DEV, TOP)

    def cold_step(accum_sum, scan_item):
        gate_weight, up_weight, down_weight, expert = scan_item
        term = routed(token_blocks, route_ids[:, :, 1:], gate_table[:, :, 1:], expert, CAP, gate_weight, up_weight, down_weight)
        return accum_sum + term, None

    accum_sum = jnp.zeros((blocks, TOK_DEV, D), jnp.float32)
    accum_sum, _ = lax.scan(cold_step, accum_sum, (w_gate, w_up, w_down, jnp.arange(EXPERTS, dtype=jnp.int32)))

    def hot_step(accum_sum, expert):
        term = routed(token_blocks, route_ids[:, :, :1], gate_table[:, :, :1], expert, HCAP, w_gate[expert], w_up[expert], w_down[expert])
        return accum_sum + term, None

    accum_sum, _ = lax.scan(hot_step, accum_sum, hot_ids)
    return accum_sum.reshape(TOKENS, D).astype(jnp.bfloat16)
```

```python
import jax
import jax.numpy as jnp
from jax import lax
from jax.experimental import pallas as pl
from jax.experimental.pallas import tpu as pltpu
from jax.sharding import PartitionSpec as P

MESH = pl.DeviceIdType.MESH
NZ = 8
SIDE = 4
SLOTS = 64
DIRS = (1, -1)
F32 = jnp.float32
BF16 = jnp.bfloat16


def kernel(
    tok_in, meta_in, wg_in, wu_in, wd_in, out_ref,
    tok, meta, wgu, wd, xs, hid, gs, pt, ybuf, part, r1, r2, r3, r4, outv,
    lsem, zs, zr, ps, pr, ts, tr, ms, mr, qs, qr, osem,
):
    dp = lax.axis_index("dp")
    ex = lax.axis_index("expert")
    z, k = dp // 2, dp % 2
    x, y = ex // SIDE, ex % SIDE

    def zdev(d):
        return (((z + d + NZ) % NZ) * 2 + k, ex)

    def xdev(d):
        return (dp, ((x + d + SIDE) % SIDE) * SIDE + y)

    def ydev(d):
        return (dp, x * SIDE + (y + d + SIDE) % SIDE)

    partner = (z * 2 + 1 - k, ex)

    def nbr(o, stage, d):
        return xdev(d) if (o + stage) % 2 == 0 else ydev(d)

    barrier = pltpu.get_barrier_semaphore()
    around = [zdev(1), zdev(-1), xdev(1), xdev(-1), ydev(1), ydev(-1), partner]
    for dev in around:
        pl.semaphore_signal(barrier, inc=1, device_id=dev, device_id_type=MESH)

    def zpiece(g, half, zz, core):
        if g < 2:
            rows = pl.multiple_of((zz * 2 + core) * 128, 128)
            return wgu.at[g, pl.ds(rows, 128), pl.ds(half * 768, 768)]
        cols = pl.multiple_of(core * 128, 128)
        return wd.at[zz, half, :, pl.ds(cols, 128)]

    local = []
    for g in range(2):
        for half, src in ((0, wg_in), (1, wu_in)):
            local.append((src.at[g], zpiece(g, half, z, k)))
    for half in range(2):
        local.append((wd_in.at[half], zpiece(2, half, z, k)))
    local.append((tok_in, tok.at[x, y]))
    local.append((meta_in, meta.at[x, y]))
    local = [pltpu.make_async_copy(s, d, lsem.at[i]) for i, (s, d) in enumerate(local)]
    for c in local:
        c.start()
    pl.semaphore_wait(barrier, len(around))
    for c in local:
        c.wait()

    sends = []

    def remote(src, dst, ssem, rsem, dev):
        return pltpu.make_async_remote_copy(
            src_ref=src, dst_ref=dst, send_sem=ssem, recv_sem=rsem,
            device_id=dev, device_id_type=MESH,
        )

    def start(*a):
        c = remote(*a)
        c.start()
        sends.append(c)

    def zsend(g, half, hop, di):
        d = DIRS[di]
        piece = zpiece(g, half, (z - d * (hop - 1) + NZ) % NZ, k)
        n = g * 7 + ((hop - 1) * 2 + half if hop < 4 else 6)
        start(piece, piece, zs.at[di, n], zr.at[di, n], zdev(d))

    def psend(g, half, zz, i):
        piece = zpiece(g, half, zz, k)
        start(piece, piece, ps.at[g, i], pr.at[g, i], partner)

    def own(g):
        for half in range(2):
            for di in range(2):
                zsend(g, half, 1, di)
        for half in range(2):
            psend(g, half, z, half)

    def pump(n):
        g, r = n // 7, n % 7
        for di in range(2):
            d = DIRS[di]
            hop, half = (r // 2 + 1, r % 2) if r < 6 else (4, di)
            zz = (z - d * hop + NZ) % NZ
            piece = zpiece(g, half, zz, k)
            remote(piece, piece, zs.at[di, n], zr.at[di, n], zdev(d)).wait_recv()
            if hop < 3 or (hop == 3 and half == di):
                zsend(g, half, hop + 1, di)
            psend(g, half, zz, 2 + di * 7 + r)
        if r == 5 and g < 2:
            own(g + 1)

    def pwait(g):
        for half in range(2):
            piece = zpiece(g, half, z, 1 - k)
            remote(piece, piece, ps.at[g, half], pr.at[g, half], partner).wait_recv()
        for r in range(7):
            for di in range(2):
                hop, half = (r // 2 + 1, r % 2) if r < 6 else (4, di)
                piece = zpiece(g, half, (z - DIRS[di] * hop + NZ) % NZ, 1 - k)
                i = 2 + di * 7 + r
                remote(piece, piece, ps.at[g, i], pr.at[g, i], partner).wait_recv()

    def major(o):
        return (x, y) if o == 0 else (y, x)

    def half_rows(di):
        return pl.ds(di * 64, 64)

    every = pl.ds(0, 128)

    def tblk(o, mi, rows):
        n = major(o)[1]
        cols = pl.ds(o * 1024, 1024)
        return tok.at[mi, n, rows, cols] if o == 0 else tok.at[n, mi, rows, cols]

    def tcol(o, ni, rows):
        cols = pl.ds(o * 1024, 1024)
        return tok.at[:, ni, rows, cols] if o == 0 else tok.at[ni, :, rows, cols]

    def w4(v):
        return (v + SIDE) % SIDE

    def tok_step(step):
        for o in range(2):
            m, n = major(o)
            for di in range(2):
                d = DIRS[di]

                def got(s, ref):
                    remote(ref, ref, ts.at[s, o, di], tr.at[s, o, di], nbr(o, s // 2, d)).wait_recv()

                if step == 1:
                    got(0, tblk(o, w4(m - d), every))
                    ref = tblk(o, w4(m - d), half_rows(di))
                elif step == 2:
                    got(1, tblk(o, w4(m - 2 * d), half_rows(di)))
                elif step == 3:
                    got(2, tcol(o, w4(n - d), every))
                    ref = tcol(o, w4(n - d), half_rows(di))
                elif step == 4:
                    got(3, tcol(o, w4(n - 2 * d), half_rows(di)))
                if step in (1, 3):
                    start(ref, ref, ts.at[step, o, di], tr.at[step, o, di], nbr(o, step // 2, d))
            if step in (0, 2):
                ref = tblk(o, m, every) if step == 0 else tcol(o, n, every)
                for di in range(2):
                    start(ref, ref, ts.at[step, o, di], tr.at[step, o, di], nbr(o, step // 2, DIRS[di]))

    def meta_step(step):
        def go(i, ref, dev):
            start(ref, ref, ms.at[i], mr.at[i], dev)

        def got(i, ref, dev):
            remote(ref, ref, ms.at[i], mr.at[i], dev).wait_recv()

        if step == 0:
            go(0, meta.at[x, y], xdev(1))
            go(1, meta.at[x, y], xdev(-1))
        elif step == 1:
            got(0, meta.at[w4(x - 1), y], xdev(1))
            go(2, meta.at[w4(x - 1), y], xdev(1))
            got(1, meta.at[w4(x + 1), y], xdev(-1))
        elif step == 2:
            got(2, meta.at[w4(x - 2), y], xdev(1))
            go(3, meta.at[:, y], ydev(1))
            go(4, meta.at[:, y], ydev(-1))
        elif step == 3:
            got(3, meta.at[:, w4(y - 1)], ydev(1))
            go(5, meta.at[:, w4(y - 1)], ydev(1))
            got(4, meta.at[:, w4(y + 1)], ydev(-1))
        else:
            got(5, meta.at[:, w4(y - 2)], ydev(1))

    own(0)
    tok_step(0)
    meta_step(0)
    pump(0)
    meta_step(1)
    tok_step(1)
    pump(1)
    meta_step(2)
    tok_step(2)
    for n in range(2, 8):
        pump(n)
        if n == 3:
            meta_step(3)
        if n == 5:
            meta_step(4)
    tok_step(3)
    for n in range(8, 11):
        pump(n)

    rows = meta[...].reshape(16, 8, 128)
    mine = [(ex * 2).astype(F32), (ex * 2 + 1).astype(F32)]
    hits, gates = [], []
    for e in range(2):
        same = [rows[:, j, :] == mine[e] for j in range(4)]
        hits.append(sum(jnp.where(s, 1.0, 0.0) for s in same))
        gates.append(sum(jnp.where(s, rows[:, 4 + j, :], 0.0) for j, s in enumerate(same)))
    hit = jnp.concatenate(hits, axis=0)
    before = lax.broadcasted_iota(jnp.int32, (128, 128), 0) < lax.broadcasted_iota(jnp.int32, (128, 128), 1)
    rank = jnp.dot(hit.astype(BF16), jnp.where(before, 1.0, 0.0).astype(BF16), preferred_element_type=F32)
    lift = jnp.where(lax.broadcasted_iota(jnp.int32, (32, 128), 0) < 16, 0.0, float(SLOTS))
    slot = jnp.where(hit > 0.5, rank + lift, -1.0)
    slot_cols = jnp.transpose(jnp.concatenate([slot, jnp.zeros((96, 128), F32)], axis=0))

    tok_step(4)
    down_i = lax.broadcasted_iota(jnp.int32, (128, 128), 0).astype(F32)
    across_i = lax.broadcasted_iota(jnp.int32, (128, 128), 1).astype(F32)
    for s in range(16):
        pick = (slot[s:s + 1] == down_i) | (slot[16 + s:17 + s] == down_i)
        gate_of = jnp.where(down_i < SLOTS, gates[0][s:s + 1], gates[1][s:s + 1])
        g_col = jnp.sum(jnp.where(pick, gate_of, 0.0), axis=1, keepdims=True)
        for e in range(2):
            gs[e, pl.ds(s * SLOTS, SLOTS), :] = g_col[e * SLOTS:(e + 1) * SLOTS]
        back = (slot_cols[:, s:s + 1] == across_i) | (slot_cols[:, 16 + s:17 + s] == across_i)
        pt[s] = jnp.where(back, 1.0, 0.0).astype(BF16)
        picked = jnp.where(pick, 1.0, 0.0).astype(BF16)
        got = jnp.dot(picked, tok[s // SIDE, s % SIDE], preferred_element_type=F32).astype(BF16)
        for e in range(2):
            xs[e, pl.ds(s * SLOTS, SLOTS), :] = got[e * SLOTS:(e + 1) * SLOTS]
        if s % 8 == 3:
            pump(11 + s // 8)

    pwait(0)

    def gate_up(e, lo, hi):
        def body(i, carry):
            r0 = pl.multiple_of((i // 3) * 512, 512)
            c0 = pl.multiple_of((i % 3) * 256, 256)
            c1 = pl.multiple_of(768 + (i % 3) * 256, 256)
            rws = xs[e, pl.ds(r0, 512), :]
            gate = jnp.dot(rws, wgu[e, :, pl.ds(c0, 256)], preferred_element_type=F32)
            up = jnp.dot(rws, wgu[e, :, pl.ds(c1, 256)], preferred_element_type=F32)
            h = gate / (1.0 + jnp.exp(-gate)) * up * gs[e, pl.ds(r0, 512), :]
            hid[e, pl.ds(r0, 512), pl.ds(c0, 256)] = h.astype(BF16)
            return carry

        lax.fori_loop(lo, hi, body, 0)

    gate_up(0, 0, 3)
    pump(13)
    gate_up(0, 3, 6)
    pump(14)
    pwait(1)
    gate_up(1, 0, 3)
    pump(15)
    pump(16)
    gate_up(1, 3, 6)
    for n in range(17, 21):
        pump(n)
    pwait(2)

    def cc(o):
        return pl.ds(o * 128, 128)

    def pblk(o, c, mi, rws):
        return part.at[c, mi, :, rws, cc(o)] if o == 0 else part.at[c, :, mi, rws, cc(o)]

    def qblk(o, c, ni, rws):
        return part.at[c, x, ni, rws, cc(o)] if o == 0 else part.at[c, ni, y, rws, cc(o)]

    def link(step, c, o, di):
        m, n = major(o)
        d = DIRS[di]
        if step == 0:
            src, dst = pblk(o, c, w4(m + 2), half_rows(di)), r1.at[c, o, di]
        elif step == 1:
            src, dst = pblk(o, c, w4(m + d), every), r2.at[c, o, di]
        elif step == 2:
            src, dst = qblk(o, c, w4(n + 2), half_rows(di)), r3.at[c, o, di]
        else:
            src, dst = qblk(o, c, w4(n + d), every), r4.at[c, o, di]
        return remote(src, dst, qs.at[step, c, o, di], qr.at[step, c, o, di], nbr(o, step // 2, d))

    def both(fn):
        for o in range(2):
            for di in range(2):
                fn(o, di)

    def plus(ref, *more):
        total = ref[...].astype(F32)
        for v in more:
            total = total + v.astype(F32)
        ref[...] = total.astype(BF16)

    def chunk(c):
        zz = (z + c) % NZ
        for e in range(2):
            yv = jnp.dot(hid[e], wd[zz, e], preferred_element_type=F32).astype(BF16)
            ybuf[:, pl.ds(e * SLOTS, SLOTS), :] = yv.reshape(16, SLOTS, 256)

        def scatter(s, carry):
            v = jnp.dot(pt[s], ybuf[s], preferred_element_type=F32).astype(BF16)
            part[c, s // SIDE, s % SIDE] = v
            return carry

        lax.fori_loop(0, 16, scatter, 0, unroll=4)
        both(lambda o, di: link(0, c, o, di).start())

    def step2(c):
        def one(o, di):
            link(0, c, o, di).wait_recv()
            m = major(o)[0]
            plus(pblk(o, c, w4(m + DIRS[di]), half_rows(di)), r1[c, o, di])
            link(1, c, o, di).start()

        both(one)

    def step3(c):
        for o in range(2):
            for di in range(2):
                link(1, c, o, di).wait_recv()
            plus(pblk(o, c, major(o)[0], every), r2[c, o, 0], r2[c, o, 1])
            for di in range(2):
                link(2, c, o, di).start()

    def step4(c):
        def one(o, di):
            link(2, c, o, di).wait_recv()
            n = major(o)[1]
            plus(qblk(o, c, w4(n + DIRS[di]), half_rows(di)), r3[c, o, di])
            link(3, c, o, di).start()

        both(one)

    def step5(c):
        zz = (z + c) % NZ
        for o in range(2):
            for di in range(2):
                link(3, c, o, di).wait_recv()
            n = major(o)[1]
            total = qblk(o, c, n, every)[...].astype(F32) + r4[c, o, 0].astype(F32) + r4[c, o, 1].astype(F32)
            col = pl.multiple_of(zz * 256 + o * 128, 128)
            outv[:, pl.ds(col, 128)] = total.astype(BF16)

    stages = (chunk, step2, step3, step4, step5)

    def turn(i, carry):
        for j, fn in enumerate(stages):
            @pl.when((i >= j) & (i < NZ + j))
            def _(j=j, fn=fn):
                fn(i - j)
        return carry

    lax.fori_loop(0, NZ + len(stages) - 1, turn, 0)

    final = pltpu.make_async_copy(outv, out_ref, osem)
    final.start()
    for c in sends:
        c.wait_send()

    def drain(c, carry):
        for step in range(4):
            both(lambda o, di: link(step, c, o, di).wait_send())
        return carry

    lax.fori_loop(0, NZ, drain, 0)
    final.wait()


def layer(tokens, expert_ids, gate_weights, hot_ids, w_gate, w_up, w_down):
    meta = jnp.concatenate([expert_ids.astype(F32), gate_weights], axis=1).T
    dma = pltpu.SemaphoreType.DMA
    any_spec = pl.BlockSpec(memory_space=pl.ANY)
    return pl.pallas_call(
        kernel,
        out_shape=jax.ShapeDtypeStruct((128, 2048), BF16),
        in_specs=[any_spec] * 5,
        out_specs=any_spec,
        scratch_shapes=[
            pltpu.VMEM((4, 4, 128, 2048), BF16),
            pltpu.VMEM((4, 4, 8, 128), F32),
            pltpu.VMEM((2, 2048, 1536), BF16),
            pltpu.VMEM((8, 2, 768, 256), BF16),
            pltpu.VMEM((2, 1024, 2048), BF16),
            pltpu.VMEM((2, 1024, 768), BF16),
            pltpu.VMEM((2, 1024, 1), F32),
            pltpu.VMEM((16, 128, 128), BF16),
            pltpu.VMEM((16, 128, 256), BF16),
            pltpu.VMEM((8, 4, 4, 128, 256), BF16),
            pltpu.VMEM((8, 2, 2, 4, 64, 128), BF16),
            pltpu.VMEM((8, 2, 2, 4, 128, 128), BF16),
            pltpu.VMEM((8, 2, 2, 64, 128), BF16),
            pltpu.VMEM((8, 2, 2, 128, 128), BF16),
            pltpu.VMEM((128, 2048), BF16),
            dma((8,)),
            dma((2, 21)), dma((2, 21)),
            dma((3, 16)), dma((3, 16)),
            dma((4, 2, 2)), dma((4, 2, 2)),
            dma((6,)), dma((6,)),
            dma((4, 8, 2, 2)), dma((4, 8, 2, 2)),
            dma,
        ],
        compiler_params=pltpu.CompilerParams(
            collective_id=0, has_side_effects=True, vmem_limit_bytes=67043328
        ),
    )(tokens, meta, w_gate, w_up, w_down)


def solution(mesh):
    placed = (
        P(("dp", "expert"), None),
        P(("dp", "expert"), None),
        P(("dp", "expert"), None),
        P(),
        P("expert", "dp", None),
        P("expert", "dp", None),
        P("expert", None, "dp"),
    )
    return jax.shard_map(
        layer, mesh=mesh, in_specs=placed, out_specs=P(("dp", "expert"), None), check_vma=False
    )
```

```python
import jax
import jax.numpy as jnp
from jax import lax
from jax.experimental import pallas as pl
from jax.experimental.pallas import tpu as pltpu
from jax.sharding import PartitionSpec as P

MESH = pl.DeviceIdType.MESH
NZ = 8
SIDE = 4
SLOTS = 64
DIRS = (1, -1)
F32 = jnp.float32
BF16 = jnp.bfloat16


def kernel(
    tok_in, ids_in, gw_in, wg_in, wu_in, wd_in, out_ref,
    tok, meta, ids, gw, wgu, wd, acc, hid, gs, pt, ybuf, part, r1, r2, r3, r4, outv,
    lsem, zs, zr, ps, pr, ts, tr, ms, mr, qs, qr, osem,
):
    dp = lax.axis_index("dp")
    ex = lax.axis_index("expert")
    z, k = dp // 2, dp % 2
    x, y = ex // SIDE, ex % SIDE

    def zdev(d):
        return (((z + d + NZ) % NZ) * 2 + k, ex)

    def xdev(d):
        return (dp, ((x + d + SIDE) % SIDE) * SIDE + y)

    def ydev(d):
        return (dp, x * SIDE + (y + d + SIDE) % SIDE)

    partner = (z * 2 + 1 - k, ex)

    def nbr(o, stage, d):
        return xdev(d) if (o + stage) % 2 == 0 else ydev(d)

    barrier = pltpu.get_barrier_semaphore()
    around = [zdev(1), zdev(-1), xdev(1), xdev(-1), ydev(1), ydev(-1), partner]
    for dev in around:
        pl.semaphore_signal(barrier, inc=1, device_id=dev, device_id_type=MESH)

    def zpiece(g, half, zz, core):
        if g < 2:
            rows = pl.multiple_of((zz * 2 + core) * 128, 128)
            return wgu.at[g, pl.ds(rows, 128), pl.ds(half * 768, 768)]
        cols = pl.multiple_of(core * 128, 128)
        return wd.at[zz, half, :, pl.ds(cols, 128)]

    local = []
    for g in range(2):
        for half, src in ((0, wg_in), (1, wu_in)):
            local.append((src.at[g], zpiece(g, half, z, k)))
    for half in range(2):
        local.append((wd_in.at[half], zpiece(2, half, z, k)))
    local.append((tok_in, tok.at[x, y]))
    local.append((ids_in, ids))
    local.append((gw_in, gw))
    local = [pltpu.make_async_copy(s, d, lsem.at[i]) for i, (s, d) in enumerate(local)]
    for c in local:
        c.start()
    for c in local[-2:]:
        c.wait()
    meta[x, y, pl.ds(0, 4)] = ids[...].astype(F32)
    meta[x, y, pl.ds(4, 4)] = gw[...]
    pl.semaphore_wait(barrier, len(around))
    for c in local[:-2]:
        c.wait()

    sends = []

    def remote(src, dst, ssem, rsem, dev):
        return pltpu.make_async_remote_copy(
            src_ref=src, dst_ref=dst, send_sem=ssem, recv_sem=rsem,
            device_id=dev, device_id_type=MESH,
        )

    def start(*a):
        c = remote(*a)
        c.start()
        sends.append(c)

    def arrival(di, r):
        return (r // 2 + 1, r % 2) if r < 6 else (4, di)

    def zdesc(g, half, hop, di):
        d = DIRS[di]
        piece = zpiece(g, half, (z - d * (hop - 1) + NZ) % NZ, k)
        n = g * 7 + ((hop - 1) * 2 + half if hop < 4 else 6)
        return remote(piece, piece, zs.at[di, n], zr.at[di, n], zdev(d))

    def pdesc(g, half, zz, i, core):
        piece = zpiece(g, half, zz, core)
        return remote(piece, piece, ps.at[g, i], pr.at[g, i], partner)

    def parrival(g, di, r, core):
        hop, half = arrival(di, r)
        return pdesc(g, half, (z - DIRS[di] * hop + NZ) % NZ, 2 + di * 7 + r, core)

    def own(g):
        for half in range(2):
            for di in range(2):
                zdesc(g, half, 1, di).start()
        for half in range(2):
            pdesc(g, half, z, half, k).start()

    def pump(n):
        g, r = n // 7, n % 7
        for di in range(2):
            d = DIRS[di]
            hop, half = arrival(di, r)
            piece = zpiece(g, half, (z - d * hop + NZ) % NZ, k)
            remote(piece, piece, zs.at[di, n], zr.at[di, n], zdev(d)).wait_recv()
            if hop < 3 or (hop == 3 and half == di):
                zdesc(g, half, hop + 1, di).start()
            parrival(g, di, r, k).start()
        if r == 5 and g < 2:
            own(g + 1)

    def pwait_own(g):
        for half in range(2):
            pdesc(g, half, z, half, 1 - k).wait_recv()

    def pwait(g, rs, dis=(0, 1)):
        for r in rs:
            for di in dis:
                parrival(g, di, r, 1 - k).wait_recv()

    def zdrain():
        for g in range(3):
            for half in range(2):
                pdesc(g, half, z, half, k).wait_send()
            for r in range(7):
                for di in range(2):
                    hop, half = arrival(di, r)
                    zdesc(g, half, hop, di).wait_send()
                    parrival(g, di, r, k).wait_send()

    def major(o):
        return (x, y) if o == 0 else (y, x)

    def half_rows(di):
        return pl.ds(di * 64, 64)

    every = pl.ds(0, 128)

    def tblk(o, mi, rows):
        n = major(o)[1]
        cols = pl.ds(o * 1024, 1024)
        return tok.at[mi, n, rows, cols] if o == 0 else tok.at[n, mi, rows, cols]

    def tcol(o, ni, rows):
        cols = pl.ds(o * 1024, 1024)
        return tok.at[:, ni, rows, cols] if o == 0 else tok.at[ni, :, rows, cols]

    def w4(v):
        return (v + SIDE) % SIDE

    def tok_step(step):
        for o in range(2):
            m, n = major(o)
            for di in range(2):
                d = DIRS[di]

                def got(s, ref):
                    remote(ref, ref, ts.at[s, o, di], tr.at[s, o, di], nbr(o, s // 2, d)).wait_recv()

                if step == 1:
                    got(0, tblk(o, w4(m - d), every))
                    ref = tblk(o, w4(m - d), half_rows(di))
                elif step == 2:
                    got(1, tblk(o, w4(m - 2 * d), half_rows(di)))
                elif step == 3:
                    got(2, tcol(o, w4(n - d), every))
                    ref = tcol(o, w4(n - d), half_rows(di))
                elif step == 4:
                    got(3, tcol(o, w4(n - 2 * d), half_rows(di)))
                if step in (1, 3):
                    start(ref, ref, ts.at[step, o, di], tr.at[step, o, di], nbr(o, step // 2, d))
            if step in (0, 2):
                ref = tblk(o, m, every) if step == 0 else tcol(o, n, every)
                for di in range(2):
                    start(ref, ref, ts.at[step, o, di], tr.at[step, o, di], nbr(o, step // 2, DIRS[di]))

    def meta_step(step):
        def go(i, ref, dev):
            start(ref, ref, ms.at[i], mr.at[i], dev)

        def got(i, ref, dev):
            remote(ref, ref, ms.at[i], mr.at[i], dev).wait_recv()

        if step == 0:
            go(0, meta.at[x, y], xdev(1))
            go(1, meta.at[x, y], xdev(-1))
        elif step == 1:
            got(0, meta.at[w4(x - 1), y], xdev(1))
            go(2, meta.at[w4(x - 1), y], xdev(1))
            got(1, meta.at[w4(x + 1), y], xdev(-1))
        elif step == 2:
            got(2, meta.at[w4(x - 2), y], xdev(1))
            go(3, meta.at[:, y], ydev(1))
            go(4, meta.at[:, y], ydev(-1))
        elif step == 3:
            got(3, meta.at[:, w4(y - 1)], ydev(1))
            go(5, meta.at[:, w4(y - 1)], ydev(1))
            got(4, meta.at[:, w4(y + 1)], ydev(-1))
        else:
            got(5, meta.at[:, w4(y - 2)], ydev(1))

    own(0)
    tok_step(0)
    meta_step(0)
    pump(0)
    meta_step(1)
    tok_step(1)
    pump(1)
    meta_step(2)
    tok_step(2)
    for n in range(2, 8):
        pump(n)
        if n == 3:
            meta_step(3)
        if n == 5:
            meta_step(4)
    tok_step(3)
    for n in range(8, 10):
        pump(n)

    rows = meta[...].reshape(16, 8, 128)
    mine = [(ex * 2).astype(F32), (ex * 2 + 1).astype(F32)]
    hits, gates = [], []
    for e in range(2):
        same = [rows[:, j, :] == mine[e] for j in range(4)]
        hits.append(sum(jnp.where(s, 1.0, 0.0) for s in same))
        gates.append(sum(jnp.where(s, rows[:, 4 + j, :], 0.0) for j, s in enumerate(same)))
    hit = jnp.concatenate(hits, axis=0)
    before = lax.broadcasted_iota(jnp.int32, (128, 128), 0) < lax.broadcasted_iota(jnp.int32, (128, 128), 1)
    rank = jnp.dot(hit.astype(BF16), jnp.where(before, 1.0, 0.0).astype(BF16), preferred_element_type=F32)
    lift = jnp.where(lax.broadcasted_iota(jnp.int32, (32, 128), 0) < 16, 0.0, float(SLOTS))
    slot = jnp.where(hit > 0.5, rank + lift, -1.0)
    slot_cols = jnp.transpose(jnp.concatenate([slot, jnp.zeros((96, 128), F32)], axis=0))

    tok_step(4)
    for c in sends:
        c.wait_send()
    down_i = lax.broadcasted_iota(jnp.int32, (128, 128), 0).astype(F32)
    across_i = lax.broadcasted_iota(jnp.int32, (128, 128), 1).astype(F32)
    for s in range(16):
        pick = (slot[s:s + 1] == down_i) | (slot[16 + s:17 + s] == down_i)
        gate_of = jnp.where(down_i < SLOTS, gates[0][s:s + 1], gates[1][s:s + 1])
        g_col = jnp.sum(jnp.where(pick, gate_of, 0.0), axis=1, keepdims=True)
        for e in range(2):
            gs[e, pl.ds(s * SLOTS, SLOTS), :] = g_col[e * SLOTS:(e + 1) * SLOTS]
        back = (slot_cols[:, s:s + 1] == across_i) | (slot_cols[:, 16 + s:17 + s] == across_i)
        pt[s] = jnp.where(back, 1.0, 0.0).astype(BF16)
        picked = jnp.where(pick, 1.0, 0.0).astype(BF16)
        got = jnp.dot(picked, tok[s // SIDE, s % SIDE], preferred_element_type=F32)
        tok[s // SIDE, s % SIDE] = got.astype(BF16)
    pump(10)
    pwait_own(0)
    pwait(0, range(7))

    def finish(e, gate, up, r0, c0):
        h = gate / (1.0 + jnp.exp(-gate)) * up * gs[e, pl.ds(r0, 512), :]
        hid[e, pl.ds(r0, 512), pl.ds(c0, 256)] = h.astype(BF16)

    def gate_up(e, offs, first, last, lo, hi):
        def body(i, carry):
            mb = i // 3
            r0 = pl.multiple_of(mb * 512, 512)
            c0 = pl.multiple_of((i % 3) * 256, 256)
            c1 = pl.multiple_of(768 + (i % 3) * 256, 256)
            who = (pl.ds(mb * 2, 2), slice(None), pl.ds(e * SLOTS, SLOTS))
            sums = [None, None]
            if offs is None:
                rws = tok[who + (slice(None),)].reshape(512, 2048)
                for j, c in enumerate((c0, c1)):
                    sums[j] = jnp.dot(rws, wgu[e, :, pl.ds(c, 256)], preferred_element_type=F32)
            else:
                for j, c in enumerate((c0, c1)):
                    total = None if first else acc[pl.ds(r0, 512), pl.ds(c, 256)]
                    for off in offs:
                        deep = pl.ds(pl.multiple_of(((z + off + NZ) % NZ) * 256, 256), 256)
                        rws = tok[who + (deep,)].reshape(512, 256)
                        term = jnp.dot(rws, wgu[e, deep, pl.ds(c, 256)], preferred_element_type=F32)
                        total = term if total is None else total + term
                    sums[j] = total
            if last:
                finish(e, sums[0], sums[1], r0, c0)
            else:
                for j, c in enumerate((c0, c1)):
                    acc[pl.ds(r0, 512), pl.ds(c, 256)] = sums[j]
            return carry

        lax.fori_loop(lo, hi, body, 0)

    gate_up(0, None, True, True, 0, 4)
    pump(11)
    gate_up(0, None, True, True, 4, 6)
    pwait_own(1)
    pwait(1, range(4))
    gate_up(1, (0, -1, 1, -2, 2), True, False, 0, 2)
    pump(12)
    gate_up(1, (0, -1, 1, -2, 2), True, False, 2, 6)
    pwait(1, (4, 5))
    gate_up(1, (-3, 3), False, False, 0, 6)
    pump(13)
    pwait(1, (6,))
    gate_up(1, (4,), False, True, 0, 6)
    pump(14)
    pwait_own(2)

    def cc(o):
        return pl.ds(o * 128, 128)

    def pblk(o, c, mi, rws):
        return part.at[c, mi, :, rws, cc(o)] if o == 0 else part.at[c, :, mi, rws, cc(o)]

    def qblk(o, c, ni, rws):
        return part.at[c, x, ni, rws, cc(o)] if o == 0 else part.at[c, ni, y, rws, cc(o)]

    def link(step, c, o, di):
        m, n = major(o)
        d = DIRS[di]
        if step == 0:
            src, dst = pblk(o, c, w4(m + 2), half_rows(di)), r1.at[c, o, di]
        elif step == 1:
            src, dst = pblk(o, c, w4(m + d), every), r2.at[c, o, di]
        elif step == 2:
            src, dst = qblk(o, c, w4(n + 2), half_rows(di)), r3.at[c, o, di]
        else:
            src, dst = qblk(o, c, w4(n + d), every), r4.at[c, o, di]
        return remote(src, dst, qs.at[step, c, o, di], qr.at[step, c, o, di], nbr(o, step // 2, d))

    def both(fn):
        for o in range(2):
            for di in range(2):
                fn(o, di)

    def plus(ref, *more):
        total = ref[...].astype(F32)
        for v in more:
            total = total + v.astype(F32)
        ref[...] = total.astype(BF16)

    def origin(c):
        near = (c + 1) // 2
        return (z + NZ + jnp.where(c % 2 == 1, -near, near)) % NZ

    def chunk(c):
        zz = origin(c)
        for e in range(2):
            yv = jnp.dot(hid[e], wd[zz, e], preferred_element_type=F32).astype(BF16)
            ybuf[:, pl.ds(e * SLOTS, SLOTS), :] = yv.reshape(16, SLOTS, 256)

        def scatter(s, carry):
            v = jnp.dot(pt[s], ybuf[s], preferred_element_type=F32).astype(BF16)
            part[c, s // SIDE, s % SIDE] = v
            return carry

        lax.fori_loop(0, 16, scatter, 0, unroll=4)
        both(lambda o, di: link(0, c, o, di).start())

    def step2(c):
        def one(o, di):
            link(0, c, o, di).wait_recv()
            m = major(o)[0]
            plus(pblk(o, c, w4(m + DIRS[di]), half_rows(di)), r1[c, o, di])
            link(1, c, o, di).start()

        both(one)

    def step3(c):
        for o in range(2):
            for di in range(2):
                link(1, c, o, di).wait_recv()
            plus(pblk(o, c, major(o)[0], every), r2[c, o, 0], r2[c, o, 1])
            for di in range(2):
                link(2, c, o, di).start()

    def step4(c):
        def one(o, di):
            link(2, c, o, di).wait_recv()
            n = major(o)[1]
            plus(qblk(o, c, w4(n + DIRS[di]), half_rows(di)), r3[c, o, di])
            link(3, c, o, di).start()

        both(one)

    def step5(c):
        zz = origin(c)
        for o in range(2):
            for di in range(2):
                link(3, c, o, di).wait_recv()
            n = major(o)[1]
            total = qblk(o, c, n, every)[...].astype(F32) + r4[c, o, 0].astype(F32) + r4[c, o, 1].astype(F32)
            col = pl.multiple_of(zz * 256 + o * 128, 128)
            outv[:, pl.ds(col, 128)] = total.astype(BF16)

    stages = (chunk, step2, step3, step4, step5)

    def weights_in(c):
        if c <= 5:
            pump(14 + c)
        if c < 7:
            hop = (c + 1) // 2
            pwait(2, (2 * hop - 2, 2 * hop - 1), ((c + 1) % 2,))
        if c == 6:
            pump(20)
        if c == 7:
            pwait(2, (6,))

    def turn(i, carry):
        for c in range(1, 8):
            @pl.when(i == c)
            def _(c=c):
                weights_in(c)
        for j, fn in enumerate(stages):
            @pl.when((i >= j) & (i < NZ + j))
            def _(j=j, fn=fn):
                fn(i - j)
        return carry

    lax.fori_loop(0, NZ + len(stages) - 1, turn, 0)

    final = pltpu.make_async_copy(outv, out_ref, osem)
    final.start()
    zdrain()

    def drain(c, carry):
        for step in range(4):
            both(lambda o, di: link(step, c, o, di).wait_send())
        return carry

    lax.fori_loop(0, NZ, drain, 0)
    final.wait()


def layer(tokens, expert_ids, gate_weights, hot_ids, w_gate, w_up, w_down):
    dma = pltpu.SemaphoreType.DMA
    any_spec = pl.BlockSpec(memory_space=pl.ANY)
    return pl.pallas_call(
        kernel,
        out_shape=jax.ShapeDtypeStruct((128, 2048), BF16),
        in_specs=[any_spec] * 6,
        out_specs=any_spec,
        scratch_shapes=[
            pltpu.VMEM((4, 4, 128, 2048), BF16),
            pltpu.VMEM((4, 4, 8, 128), F32),
            pltpu.VMEM((4, 128), jnp.int32),
            pltpu.VMEM((4, 128), F32),
            pltpu.VMEM((2, 2048, 1536), BF16),
            pltpu.VMEM((8, 2, 768, 256), BF16),
            pltpu.VMEM((1024, 1536), F32),
            pltpu.VMEM((2, 1024, 768), BF16),
            pltpu.VMEM((2, 1024, 1), F32),
            pltpu.VMEM((16, 128, 128), BF16),
            pltpu.VMEM((16, 128, 256), BF16),
            pltpu.VMEM((8, 4, 4, 128, 256), BF16),
            pltpu.VMEM((8, 2, 2, 4, 64, 128), BF16),
            pltpu.VMEM((8, 2, 2, 4, 128, 128), BF16),
            pltpu.VMEM((8, 2, 2, 64, 128), BF16),
            pltpu.VMEM((8, 2, 2, 128, 128), BF16),
            pltpu.VMEM((128, 2048), BF16),
            dma((9,)),
            dma((2, 21)), dma((2, 21)),
            dma((3, 16)), dma((3, 16)),
            dma((4, 2, 2)), dma((4, 2, 2)),
            dma((6,)), dma((6,)),
            dma((4, 8, 2, 2)), dma((4, 8, 2, 2)),
            dma,
        ],
        compiler_params=pltpu.CompilerParams(
            collective_id=0, has_side_effects=True, vmem_limit_bytes=67043328
        ),
    )(tokens, expert_ids.T, gate_weights.T, w_gate, w_up, w_down)


def solution(mesh):
    placed = (
        P(("dp", "expert"), None),
        P(("dp", "expert"), None),
        P(("dp", "expert"), None),
        P(),
        P("expert", "dp", None),
        P("expert", "dp", None),
        P("expert", None, "dp"),
    )
    return jax.shard_map(
        layer, mesh=mesh, in_specs=placed, out_specs=P(("dp", "expert"), None), check_vma=False
    )
```

```python
import jax
import jax.numpy as jnp
from jax import lax
from jax.experimental import pallas as pl
from jax.experimental.pallas import tpu as pltpu
from jax.sharding import PartitionSpec as P

MESH = pl.DeviceIdType.MESH
NZ = 8
SIDE = 4
SLOTS = 64
DIRS = (1, -1)
NEAR = ((0, 0), (1, 0), (-1, 0), (0, 1), (0, -1), (1, 1), (1, -1), (-1, 1))
FAR = ((-1, -1), (2, 0), (2, 1), (2, -1), (0, 2), (1, 2), (-1, 2), (2, 2))
SOURCES = NEAR + FAR
F32 = jnp.float32
BF16 = jnp.bfloat16


def kernel(
    tok_in, ids_in, gw_in, wg_in, wu_in, wd_in, out_ref,
    tok, meta, ids, gw, wgu, wd, acc, hid, gs, pt, ybuf, part, r1, r2, r3, r4, outv,
    lsem, zs, zr, ps, pr, ts, tr, ms, mr, qs, qr, osem,
):
    dp = lax.axis_index("dp")
    ex = lax.axis_index("expert")
    z, k = dp // 2, dp % 2
    x, y = ex // SIDE, ex % SIDE

    def zdev(d):
        return (((z + d + NZ) % NZ) * 2 + k, ex)

    def xdev(d):
        return (dp, ((x + d + SIDE) % SIDE) * SIDE + y)

    def ydev(d):
        return (dp, x * SIDE + (y + d + SIDE) % SIDE)

    partner = (z * 2 + 1 - k, ex)

    def nbr(o, stage, d):
        return xdev(d) if (o + stage) % 2 == 0 else ydev(d)

    barrier = pltpu.get_barrier_semaphore()
    around = [zdev(1), zdev(-1), xdev(1), xdev(-1), ydev(1), ydev(-1), partner]
    for dev in around:
        pl.semaphore_signal(barrier, inc=1, device_id=dev, device_id_type=MESH)

    def zpiece(g, half, zz, core):
        if g < 2:
            rows = pl.multiple_of((zz * 2 + core) * 128, 128)
            return wgu.at[g, pl.ds(rows, 128), pl.ds(half * 768, 768)]
        cols = pl.multiple_of(core * 128, 128)
        return wd.at[zz, half, :, pl.ds(cols, 128)]

    local = []
    for g in range(2):
        for half, src in ((0, wg_in), (1, wu_in)):
            local.append((src.at[g], zpiece(g, half, z, k)))
    for half in range(2):
        local.append((wd_in.at[half], zpiece(2, half, z, k)))
    local.append((tok_in, tok.at[x, y]))
    local.append((ids_in, ids))
    local.append((gw_in, gw))
    local = [pltpu.make_async_copy(s, d, lsem.at[i]) for i, (s, d) in enumerate(local)]
    for c in local:
        c.start()
    for c in local[-2:]:
        c.wait()
    meta[x, y, pl.ds(0, 4)] = ids[...].astype(F32)
    meta[x, y, pl.ds(4, 4)] = gw[...]
    pl.semaphore_wait(barrier, len(around))
    for c in local[:-2]:
        c.wait()

    sends = []

    def remote(src, dst, ssem, rsem, dev):
        return pltpu.make_async_remote_copy(
            src_ref=src, dst_ref=dst, send_sem=ssem, recv_sem=rsem,
            device_id=dev, device_id_type=MESH,
        )

    def start(*a):
        c = remote(*a)
        c.start()
        sends.append(c)

    def arrival(di, r):
        return (r // 2 + 1, r % 2) if r < 6 else (4, di)

    def zdesc(g, half, hop, di):
        d = DIRS[di]
        piece = zpiece(g, half, (z - d * (hop - 1) + NZ) % NZ, k)
        n = g * 7 + ((hop - 1) * 2 + half if hop < 4 else 6)
        return remote(piece, piece, zs.at[di, n], zr.at[di, n], zdev(d))

    def pdesc(g, half, zz, i, core):
        piece = zpiece(g, half, zz, core)
        return remote(piece, piece, ps.at[g, i], pr.at[g, i], partner)

    def parrival(g, di, r, core):
        hop, half = arrival(di, r)
        return pdesc(g, half, (z - DIRS[di] * hop + NZ) % NZ, 2 + di * 7 + r, core)

    def own(g):
        for half in range(2):
            for di in range(2):
                zdesc(g, half, 1, di).start()
        for half in range(2):
            pdesc(g, half, z, half, k).start()

    def pump(n):
        g, r = n // 7, n % 7
        for di in range(2):
            d = DIRS[di]
            hop, half = arrival(di, r)
            piece = zpiece(g, half, (z - d * hop + NZ) % NZ, k)
            remote(piece, piece, zs.at[di, n], zr.at[di, n], zdev(d)).wait_recv()
            if hop < 3 or (hop == 3 and half == di):
                zdesc(g, half, hop + 1, di).start()
            parrival(g, di, r, k).start()
        if r == 5 and g < 2:
            own(g + 1)

    def pwait_own(g):
        for half in range(2):
            pdesc(g, half, z, half, 1 - k).wait_recv()

    def pwait(g, rs, dis=(0, 1)):
        for r in rs:
            for di in dis:
                parrival(g, di, r, 1 - k).wait_recv()

    def zdrain():
        for g in range(3):
            for half in range(2):
                pdesc(g, half, z, half, k).wait_send()
            for r in range(7):
                for di in range(2):
                    hop, half = arrival(di, r)
                    zdesc(g, half, hop, di).wait_send()
                    parrival(g, di, r, k).wait_send()

    def major(o):
        return (x, y) if o == 0 else (y, x)

    def half_rows(di):
        return pl.ds(di * 64, 64)

    every = pl.ds(0, 128)

    def tblk(o, mi, rows):
        n = major(o)[1]
        cols = pl.ds(o * 1024, 1024)
        return tok.at[mi, n, rows, cols] if o == 0 else tok.at[n, mi, rows, cols]

    def tcol(o, ni, rows):
        cols = pl.ds(o * 1024, 1024)
        return tok.at[:, ni, rows, cols] if o == 0 else tok.at[ni, :, rows, cols]

    def w4(v):
        return (v + SIDE) % SIDE

    def tok_step(step):
        for o in range(2):
            m, n = major(o)
            for di in range(2):
                d = DIRS[di]

                def got(s, ref):
                    remote(ref, ref, ts.at[s, o, di], tr.at[s, o, di], nbr(o, s // 2, d)).wait_recv()

                if step == 1:
                    got(0, tblk(o, w4(m - d), every))
                    ref = tblk(o, w4(m - d), half_rows(di))
                elif step == 2:
                    got(1, tblk(o, w4(m - 2 * d), half_rows(di)))
                elif step == 3:
                    got(2, tcol(o, w4(n - d), every))
                    ref = tcol(o, w4(n - d), half_rows(di))
                elif step == 4:
                    got(3, tcol(o, w4(n - 2 * d), half_rows(di)))
                if step in (1, 3):
                    start(ref, ref, ts.at[step, o, di], tr.at[step, o, di], nbr(o, step // 2, d))
            if step in (0, 2):
                ref = tblk(o, m, every) if step == 0 else tcol(o, n, every)
                for di in range(2):
                    start(ref, ref, ts.at[step, o, di], tr.at[step, o, di], nbr(o, step // 2, DIRS[di]))

    def meta_step(step):
        def go(i, ref, dev):
            start(ref, ref, ms.at[i], mr.at[i], dev)

        def got(i, ref, dev):
            remote(ref, ref, ms.at[i], mr.at[i], dev).wait_recv()

        if step == 0:
            go(0, meta.at[x, y], xdev(1))
            go(1, meta.at[x, y], xdev(-1))
        elif step == 1:
            got(0, meta.at[w4(x - 1), y], xdev(1))
            go(2, meta.at[w4(x - 1), y], xdev(1))
            got(1, meta.at[w4(x + 1), y], xdev(-1))
        elif step == 2:
            got(2, meta.at[w4(x - 2), y], xdev(1))
            go(3, meta.at[:, y], ydev(1))
            go(4, meta.at[:, y], ydev(-1))
        elif step == 3:
            got(3, meta.at[:, w4(y - 1)], ydev(1))
            go(5, meta.at[:, w4(y - 1)], ydev(1))
            got(4, meta.at[:, w4(y + 1)], ydev(-1))
        else:
            got(5, meta.at[:, w4(y - 2)], ydev(1))

    own(0)
    tok_step(0)
    meta_step(0)
    pump(0)
    meta_step(1)
    tok_step(1)
    pump(1)
    meta_step(2)
    tok_step(2)
    for n in range(2, 8):
        pump(n)
        if n == 3:
            meta_step(3)
        if n == 5:
            meta_step(4)
    tok_step(3)

    def source(q):
        return w4(x + SOURCES[q][0]), w4(y + SOURCES[q][1])

    rows = jnp.stack([meta[source(q)] for q in range(16)])
    mine = [(ex * 2).astype(F32), (ex * 2 + 1).astype(F32)]
    hits, gates = [], []
    for e in range(2):
        same = [rows[:, j, :] == mine[e] for j in range(4)]
        hits.append(sum(jnp.where(s, 1.0, 0.0) for s in same))
        gates.append(sum(jnp.where(s, rows[:, 4 + j, :], 0.0) for j, s in enumerate(same)))
    hit = jnp.concatenate(hits, axis=0)
    before = lax.broadcasted_iota(jnp.int32, (128, 128), 0) < lax.broadcasted_iota(jnp.int32, (128, 128), 1)
    rank = jnp.dot(hit.astype(BF16), jnp.where(before, 1.0, 0.0).astype(BF16), preferred_element_type=F32)
    lift = jnp.where(lax.broadcasted_iota(jnp.int32, (32, 128), 0) < 16, 0.0, float(SLOTS))
    slot = jnp.where(hit > 0.5, rank + lift, -1.0)
    slot_cols = jnp.transpose(jnp.concatenate([slot, jnp.zeros((96, 128), F32)], axis=0))

    down_i = lax.broadcasted_iota(jnp.int32, (128, 128), 0).astype(F32)
    across_i = lax.broadcasted_iota(jnp.int32, (128, 128), 1).astype(F32)

    def gather(qs_):
        for q in qs_:
            pick = (slot[q:q + 1] == down_i) | (slot[16 + q:17 + q] == down_i)
            gate_of = jnp.where(down_i < SLOTS, gates[0][q:q + 1], gates[1][q:q + 1])
            g_col = jnp.sum(jnp.where(pick, gate_of, 0.0), axis=1, keepdims=True)
            for e in range(2):
                gs[e, pl.ds(q * SLOTS, SLOTS), :] = g_col[e * SLOTS:(e + 1) * SLOTS]
            back = (slot_cols[:, q:q + 1] == across_i) | (slot_cols[:, 16 + q:17 + q] == across_i)
            pt[q] = jnp.where(back, 1.0, 0.0).astype(BF16)
            picked = jnp.where(pick, 1.0, 0.0).astype(BF16)
            got = jnp.dot(picked, tok[source(q)], preferred_element_type=F32).astype(BF16)
            for c in range(NZ):
                part[c, q // SIDE, q % SIDE] = got[:, c * 256:(c + 1) * 256]

    def gate_up(e, offs, first, last, lo, hi):
        def body(i, carry):
            mb = i // 3
            r0 = pl.multiple_of(mb * 512, 512)
            c0 = pl.multiple_of((i % 3) * 256, 256)
            c1 = pl.multiple_of(768 + (i % 3) * 256, 256)
            deep = range(NZ) if offs is None else [(z + off + NZ) % NZ for off in offs]
            rws = jnp.concatenate(
                [part[c, pl.ds(mb * 2, 2), :, pl.ds(e * SLOTS, SLOTS), :].reshape(512, 256) for c in deep], axis=1
            )
            sums = []
            for col in (c0, c1):
                w = jnp.concatenate(
                    [wgu[e, pl.ds(pl.multiple_of(c * 256, 256), 256), pl.ds(col, 256)] for c in deep], axis=0
                )
                total = jnp.dot(rws, w, preferred_element_type=F32)
                sums.append(total if first else total + acc[pl.ds(r0, 512), pl.ds(col, 256)])
            if last:
                gate, up = sums
                h = gate / (1.0 + jnp.exp(-gate)) * up * gs[e, pl.ds(r0, 512), :]
                hid[e, pl.ds(r0, 512), pl.ds(c0, 256)] = h.astype(BF16)
            else:
                for col, total in zip((c0, c1), sums):
                    acc[pl.ds(r0, 512), pl.ds(col, 256)] = total
            return carry

        lax.fori_loop(lo, hi, body, 0)

    soon = (0, -1, 1, -2, 2)
    gather(range(8))
    pwait_own(0)
    pwait(0, range(7))
    gate_up(0, None, True, True, 0, 2)
    pump(8)
    gate_up(0, None, True, True, 2, 3)
    pump(9)
    tok_step(4)
    gather(range(8, 16))
    pump(10)
    gate_up(0, None, True, True, 3, 6)
    pump(11)
    pwait_own(1)
    pwait(1, range(4))
    gate_up(1, soon, True, False, 0, 4)
    pump(12)
    gate_up(1, soon, True, False, 4, 6)
    pwait(1, (4, 5))
    gate_up(1, (-3, 3), False, False, 0, 6)
    pump(13)
    pwait(1, (6,))
    gate_up(1, (4,), False, True, 0, 6)
    pwait_own(2)

    def cc(o):
        return pl.ds(o * 128, 128)

    def pblk(o, c, mi, rws):
        return part.at[c, mi, :, rws, cc(o)] if o == 0 else part.at[c, :, mi, rws, cc(o)]

    def qblk(o, c, ni, rws):
        return part.at[c, x, ni, rws, cc(o)] if o == 0 else part.at[c, ni, y, rws, cc(o)]

    def link(step, c, o, di):
        m, n = major(o)
        d = DIRS[di]
        if step == 0:
            src, dst = pblk(o, c, w4(m + 2), half_rows(di)), r1.at[c, o, di]
        elif step == 1:
            src, dst = pblk(o, c, w4(m + d), every), r2.at[c, o, di]
        elif step == 2:
            src, dst = qblk(o, c, w4(n + 2), half_rows(di)), r3.at[c, o, di]
        else:
            src, dst = qblk(o, c, w4(n + d), every), r4.at[c, o, di]
        return remote(src, dst, qs.at[step, c, o, di], qr.at[step, c, o, di], nbr(o, step // 2, d))

    def both(fn):
        for o in range(2):
            for di in range(2):
                fn(o, di)

    def plus(ref, *more):
        total = ref[...].astype(F32)
        for v in more:
            total = total + v.astype(F32)
        ref[...] = total.astype(BF16)

    def origin(c):
        near = (c + 1) // 2
        return (z + NZ + jnp.where(c % 2 == 1, -near, near)) % NZ

    def chunk(c):
        zz = origin(c)
        for e in range(2):
            yv = jnp.dot(hid[e], wd[zz, e], preferred_element_type=F32).astype(BF16)
            ybuf[:, pl.ds(e * SLOTS, SLOTS), :] = yv.reshape(16, SLOTS, 256)

        for q in range(16):
            v = jnp.dot(pt[q], ybuf[q], preferred_element_type=F32).astype(BF16)
            sx, sy = source(q)
            part[c, sx, sy] = v
        both(lambda o, di: link(0, c, o, di).start())

    def step2(c):
        def one(o, di):
            link(0, c, o, di).wait_recv()
            m = major(o)[0]
            plus(pblk(o, c, w4(m + DIRS[di]), half_rows(di)), r1[c, o, di])
            link(1, c, o, di).start()

        both(one)

    def step3(c):
        for o in range(2):
            for di in range(2):
                link(1, c, o, di).wait_recv()
            plus(pblk(o, c, major(o)[0], every), r2[c, o, 0], r2[c, o, 1])
            for di in range(2):
                link(2, c, o, di).start()

    def step4(c):
        def one(o, di):
            link(2, c, o, di).wait_recv()
            n = major(o)[1]
            plus(qblk(o, c, w4(n + DIRS[di]), half_rows(di)), r3[c, o, di])
            link(3, c, o, di).start()

        both(one)

    def step5(c):
        zz = origin(c)
        for o in range(2):
            for di in range(2):
                link(3, c, o, di).wait_recv()
            n = major(o)[1]
            total = qblk(o, c, n, every)[...].astype(F32) + r4[c, o, 0].astype(F32) + r4[c, o, 1].astype(F32)
            col = pl.multiple_of(zz * 256 + o * 128, 128)
            outv[:, pl.ds(col, 128)] = total.astype(BF16)

    stages = ((0, chunk), (1, step2), (3, step3), (5, step4), (7, step5))

    def weights_in(c):
        if c == 1:
            pump(14)
        if c <= 5:
            pump(14 + c)
        if c < 7:
            hop = (c + 1) // 2
            pwait(2, (2 * hop - 2, 2 * hop - 1), ((c + 1) % 2,))
        if c == 6:
            pump(20)
        if c == 7:
            pwait(2, (6,))

    def turn(i, carry):
        for c in range(1, 8):
            @pl.when(i == c)
            def _(c=c):
                weights_in(c)
        for j, fn in stages:
            @pl.when((i >= j) & (i < NZ + j))
            def _(j=j, fn=fn):
                fn(i - j)
        return carry

    lax.fori_loop(0, NZ + stages[-1][0], turn, 0)

    final = pltpu.make_async_copy(outv, out_ref, osem)
    final.start()
    for c in sends:
        c.wait_send()
    zdrain()

    def drain(c, carry):
        for step in range(4):
            both(lambda o, di: link(step, c, o, di).wait_send())
        return carry

    lax.fori_loop(0, NZ, drain, 0)
    final.wait()


def layer(tokens, expert_ids, gate_weights, hot_ids, w_gate, w_up, w_down):
    dma = pltpu.SemaphoreType.DMA
    any_spec = pl.BlockSpec(memory_space=pl.ANY)
    return pl.pallas_call(
        kernel,
        out_shape=jax.ShapeDtypeStruct((128, 2048), BF16),
        in_specs=[any_spec] * 6,
        out_specs=any_spec,
        scratch_shapes=[
            pltpu.VMEM((4, 4, 128, 2048), BF16),
            pltpu.VMEM((4, 4, 8, 128), F32),
            pltpu.VMEM((4, 128), jnp.int32),
            pltpu.VMEM((4, 128), F32),
            pltpu.VMEM((2, 2048, 1536), BF16),
            pltpu.VMEM((8, 2, 768, 256), BF16),
            pltpu.VMEM((1024, 1536), F32),
            pltpu.VMEM((2, 1024, 768), BF16),
            pltpu.VMEM((2, 1024, 1), F32),
            pltpu.VMEM((16, 128, 128), BF16),
            pltpu.VMEM((16, 128, 256), BF16),
            pltpu.VMEM((8, 4, 4, 128, 256), BF16),
            pltpu.VMEM((8, 2, 2, 4, 64, 128), BF16),
            pltpu.VMEM((8, 2, 2, 4, 128, 128), BF16),
            pltpu.VMEM((8, 2, 2, 64, 128), BF16),
            pltpu.VMEM((8, 2, 2, 128, 128), BF16),
            pltpu.VMEM((128, 2048), BF16),
            dma((9,)),
            dma((2, 21)), dma((2, 21)),
            dma((3, 16)), dma((3, 16)),
            dma((4, 2, 2)), dma((4, 2, 2)),
            dma((6,)), dma((6,)),
            dma((4, 8, 2, 2)), dma((4, 8, 2, 2)),
            dma,
        ],
        compiler_params=pltpu.CompilerParams(
            collective_id=0, has_side_effects=True, vmem_limit_bytes=67043328
        ),
    )(tokens, expert_ids.T, gate_weights.T, w_gate, w_up, w_down)


def solution(mesh):
    placed = (
        P(("dp", "expert"), None),
        P(("dp", "expert"), None),
        P(("dp", "expert"), None),
        P(),
        P("expert", "dp", None),
        P("expert", "dp", None),
        P("expert", None, "dp"),
    )
    return jax.shard_map(
        layer, mesh=mesh, in_specs=placed, out_specs=P(("dp", "expert"), None), check_vma=False
    )
```

```python
import jax
import jax.numpy as jnp
from jax import lax
from jax.experimental import pallas as pl
from jax.experimental.pallas import tpu as pltpu
from jax.sharding import PartitionSpec as P

MESH = pl.DeviceIdType.MESH
NZ = 8
SIDE = 4
SLOTS = 64
DIRS = (1, -1)
NEAR = ((0, 0), (1, 0), (-1, 0), (0, 1), (0, -1), (1, 1), (1, -1), (-1, 1))
FAR = ((-1, -1), (2, 0), (2, 1), (2, -1), (0, 2), (1, 2), (-1, 2), (2, 2))
SOURCES = NEAR + FAR
F32 = jnp.float32
BF16 = jnp.bfloat16


def kernel(
    tok_in, ids_in, gw_in, wg_in, wu_in, wd_in, out_ref,
    tok, meta, ids, gw, wgu, wd, acc, hid, gs, pt, ybuf, part, r1, r2, r3, r4, outv,
    lsem, zs, zr, ps, pr, ts, tr, ms, mr, qs, qr, osem,
):
    dp = lax.axis_index("dp")
    ex = lax.axis_index("expert")
    z, k = dp // 2, dp % 2
    x, y = ex // SIDE, ex % SIDE

    def zdev(d):
        return (((z + d + NZ) % NZ) * 2 + k, ex)

    def xdev(d):
        return (dp, ((x + d + SIDE) % SIDE) * SIDE + y)

    def ydev(d):
        return (dp, x * SIDE + (y + d + SIDE) % SIDE)

    partner = (z * 2 + 1 - k, ex)

    def nbr(o, stage, d):
        return xdev(d) if (o + stage) % 2 == 0 else ydev(d)

    barrier = pltpu.get_barrier_semaphore()
    around = [zdev(1), zdev(-1), xdev(1), xdev(-1), ydev(1), ydev(-1), partner]
    for dev in around:
        pl.semaphore_signal(barrier, inc=1, device_id=dev, device_id_type=MESH)

    def zpiece(g, half, zz, core):
        if g < 2:
            rows = pl.multiple_of((zz * 2 + core) * 128, 128)
            return wgu.at[g, pl.ds(rows, 128), pl.ds(half * 768, 768)]
        cols = pl.multiple_of(core * 128, 128)
        return wd.at[zz, half, :, pl.ds(cols, 128)]

    local = []
    for g in range(2):
        for half, src in ((0, wg_in), (1, wu_in)):
            local.append((src.at[g], zpiece(g, half, z, k)))
    for half in range(2):
        local.append((wd_in.at[half], zpiece(2, half, z, k)))
    local.append((tok_in, tok.at[x, y]))
    local.append((ids_in, ids))
    local.append((gw_in, gw))
    local = [pltpu.make_async_copy(s, d, lsem.at[i]) for i, (s, d) in enumerate(local)]
    for c in local:
        c.start()
    for c in local[-2:]:
        c.wait()
    meta[x, y, pl.ds(0, 4)] = ids[...].astype(F32)
    meta[x, y, pl.ds(4, 4)] = gw[...]
    pl.semaphore_wait(barrier, len(around))
    for c in local[:-2]:
        c.wait()

    sends = []

    def remote(src, dst, ssem, rsem, dev):
        return pltpu.make_async_remote_copy(
            src_ref=src, dst_ref=dst, send_sem=ssem, recv_sem=rsem,
            device_id=dev, device_id_type=MESH,
        )

    def start(*a):
        c = remote(*a)
        c.start()
        sends.append(c)

    def arrival(di, r):
        return (r // 2 + 1, r % 2) if r < 6 else (4, di)

    def zdesc(g, half, hop, di):
        d = DIRS[di]
        piece = zpiece(g, half, (z - d * (hop - 1) + NZ) % NZ, k)
        n = g * 7 + ((hop - 1) * 2 + half if hop < 4 else 6)
        return remote(piece, piece, zs.at[di, n], zr.at[di, n], zdev(d))

    def pdesc(g, half, zz, i, core):
        piece = zpiece(g, half, zz, core)
        return remote(piece, piece, ps.at[g, i], pr.at[g, i], partner)

    def parrival(g, di, r, core):
        hop, half = arrival(di, r)
        return pdesc(g, half, (z - DIRS[di] * hop + NZ) % NZ, 2 + di * 7 + r, core)

    def own(g):
        for half in range(2):
            for di in range(2):
                zdesc(g, half, 1, di).start()
        for half in range(2):
            pdesc(g, half, z, half, k).start()

    def pump(n):
        g, r = n // 7, n % 7
        for di in range(2):
            d = DIRS[di]
            hop, half = arrival(di, r)
            piece = zpiece(g, half, (z - d * hop + NZ) % NZ, k)
            remote(piece, piece, zs.at[di, n], zr.at[di, n], zdev(d)).wait_recv()
            if hop < 3 or (hop == 3 and half == di):
                zdesc(g, half, hop + 1, di).start()
            parrival(g, di, r, k).start()
        if r == 5 and g < 2:
            own(g + 1)

    def pwait_own(g):
        for half in range(2):
            pdesc(g, half, z, half, 1 - k).wait_recv()

    def pwait(g, rs, dis=(0, 1)):
        for r in rs:
            for di in dis:
                parrival(g, di, r, 1 - k).wait_recv()

    def zdrain():
        for g in range(3):
            for half in range(2):
                pdesc(g, half, z, half, k).wait_send()
            for r in range(7):
                for di in range(2):
                    hop, half = arrival(di, r)
                    zdesc(g, half, hop, di).wait_send()
                    parrival(g, di, r, k).wait_send()

    def major(o):
        return (x, y) if o == 0 else (y, x)

    def half_rows(di):
        return pl.ds(di * 64, 64)

    every = pl.ds(0, 128)

    def tblk(o, mi, rows):
        n = major(o)[1]
        cols = pl.ds(o * 1024, 1024)
        return tok.at[mi, n, rows, cols] if o == 0 else tok.at[n, mi, rows, cols]

    def tcol(o, ni, rows):
        cols = pl.ds(o * 1024, 1024)
        return tok.at[:, ni, rows, cols] if o == 0 else tok.at[ni, :, rows, cols]

    def w4(v):
        return (v + SIDE) % SIDE

    def tok_step(step):
        for o in range(2):
            m, n = major(o)
            for di in range(2):
                d = DIRS[di]

                def got(s, ref):
                    remote(ref, ref, ts.at[s, o, di], tr.at[s, o, di], nbr(o, s // 2, d)).wait_recv()

                if step == 1:
                    got(0, tblk(o, w4(m - d), every))
                    ref = tblk(o, w4(m - d), half_rows(di))
                elif step == 2:
                    got(1, tblk(o, w4(m - 2 * d), half_rows(di)))
                elif step == 3:
                    got(2, tcol(o, w4(n - d), every))
                    ref = tcol(o, w4(n - d), half_rows(di))
                elif step == 4:
                    got(3, tcol(o, w4(n - 2 * d), half_rows(di)))
                if step in (1, 3):
                    start(ref, ref, ts.at[step, o, di], tr.at[step, o, di], nbr(o, step // 2, d))
            if step in (0, 2):
                ref = tblk(o, m, every) if step == 0 else tcol(o, n, every)
                for di in range(2):
                    start(ref, ref, ts.at[step, o, di], tr.at[step, o, di], nbr(o, step // 2, DIRS[di]))

    def meta_step(step):
        def go(i, ref, dev):
            start(ref, ref, ms.at[i], mr.at[i], dev)

        def got(i, ref, dev):
            remote(ref, ref, ms.at[i], mr.at[i], dev).wait_recv()

        if step == 0:
            go(0, meta.at[x, y], xdev(1))
            go(1, meta.at[x, y], xdev(-1))
        elif step == 1:
            got(0, meta.at[w4(x - 1), y], xdev(1))
            go(2, meta.at[w4(x - 1), y], xdev(1))
            got(1, meta.at[w4(x + 1), y], xdev(-1))
        elif step == 2:
            got(2, meta.at[w4(x - 2), y], xdev(1))
            go(3, meta.at[:, y], ydev(1))
            go(4, meta.at[:, y], ydev(-1))
        elif step == 3:
            got(3, meta.at[:, w4(y - 1)], ydev(1))
            go(5, meta.at[:, w4(y - 1)], ydev(1))
            got(4, meta.at[:, w4(y + 1)], ydev(-1))
        else:
            got(5, meta.at[:, w4(y - 2)], ydev(1))

    own(0)
    tok_step(0)
    meta_step(0)
    pump(0)
    meta_step(1)
    tok_step(1)
    pump(1)
    meta_step(2)
    tok_step(2)
    for n in range(2, 8):
        pump(n)
        if n == 3:
            meta_step(3)
        if n == 5:
            meta_step(4)
    tok_step(3)

    def source(q):
        return w4(x + SOURCES[q][0]), w4(y + SOURCES[q][1])

    rows = jnp.stack([meta[source(q)] for q in range(16)])
    mine = [(ex * 2).astype(F32), (ex * 2 + 1).astype(F32)]
    hits, gates = [], []
    for e in range(2):
        same = [rows[:, j, :] == mine[e] for j in range(4)]
        hits.append(sum(jnp.where(s, 1.0, 0.0) for s in same))
        gates.append(sum(jnp.where(s, rows[:, 4 + j, :], 0.0) for j, s in enumerate(same)))
    hit = jnp.concatenate(hits, axis=0)
    before = lax.broadcasted_iota(jnp.int32, (128, 128), 0) < lax.broadcasted_iota(jnp.int32, (128, 128), 1)
    rank = jnp.dot(hit.astype(BF16), jnp.where(before, 1.0, 0.0).astype(BF16), preferred_element_type=F32)
    lift = jnp.where(lax.broadcasted_iota(jnp.int32, (32, 128), 0) < 16, 0.0, float(SLOTS))
    slot = jnp.where(hit > 0.5, rank + lift, -1.0)
    slot_cols = jnp.transpose(jnp.concatenate([slot, jnp.zeros((96, 128), F32)], axis=0))

    down_i = lax.broadcasted_iota(jnp.int32, (128, 128), 0).astype(F32)
    across_i = lax.broadcasted_iota(jnp.int32, (128, 128), 1).astype(F32)

    def gather(qs_):
        for q in qs_:
            pick = (slot[q:q + 1] == down_i) | (slot[16 + q:17 + q] == down_i)
            gate_of = jnp.where(down_i < SLOTS, gates[0][q:q + 1], gates[1][q:q + 1])
            g_col = jnp.sum(jnp.where(pick, gate_of, 0.0), axis=1, keepdims=True)
            for e in range(2):
                gs[e, pl.ds(q * SLOTS, SLOTS), :] = g_col[e * SLOTS:(e + 1) * SLOTS]
            back = (slot_cols[:, q:q + 1] == across_i) | (slot_cols[:, 16 + q:17 + q] == across_i)
            pt[q] = jnp.where(back, 1.0, 0.0).astype(BF16)
            picked = jnp.where(pick, 1.0, 0.0).astype(BF16)
            got = jnp.dot(picked, tok[source(q)], preferred_element_type=F32).astype(BF16)
            for c in range(NZ):
                part[c, q // SIDE, q % SIDE] = got[:, c * 256:(c + 1) * 256]

    def gate_up(e, offs, first, last, lo, hi):
        def body(i, carry):
            mb = i // 3
            r0 = pl.multiple_of(mb * 512, 512)
            c0 = pl.multiple_of((i % 3) * 256, 256)
            c1 = pl.multiple_of(768 + (i % 3) * 256, 256)
            deep = range(NZ) if offs is None else [(z + off + NZ) % NZ for off in offs]
            rws = jnp.concatenate(
                [part[c, pl.ds(mb * 2, 2), :, pl.ds(e * SLOTS, SLOTS), :].reshape(512, 256) for c in deep], axis=1
            )
            sums = []
            for col in (c0, c1):
                w = jnp.concatenate(
                    [wgu[e, pl.ds(pl.multiple_of(c * 256, 256), 256), pl.ds(col, 256)] for c in deep], axis=0
                )
                total = jnp.dot(rws, w, preferred_element_type=F32)
                sums.append(total if first else total + acc[pl.ds(r0, 512), pl.ds(col, 256)])
            if last:
                gate, up = sums
                h = gate / (1.0 + jnp.exp(-gate)) * up * gs[e, pl.ds(r0, 512), :]
                hid[e, pl.ds(r0, 512), pl.ds(c0, 256)] = h.astype(BF16)
            else:
                for col, total in zip((c0, c1), sums):
                    acc[pl.ds(r0, 512), pl.ds(col, 256)] = total
            return carry

        lax.fori_loop(lo, hi, body, 0)

    soon = (0, -1, 1, -2, 2)
    gather(range(8))
    pwait_own(0)
    pwait(0, range(7))
    gate_up(0, None, True, True, 0, 2)
    pump(8)
    gate_up(0, None, True, True, 2, 3)
    pump(9)
    tok_step(4)
    gather(range(8, 16))
    pump(10)
    gate_up(0, None, True, True, 3, 6)
    pump(11)
    pwait_own(1)
    pwait(1, range(4))
    gate_up(1, soon, True, False, 0, 4)
    pump(12)
    gate_up(1, soon, True, False, 4, 6)
    pwait(1, (4, 5))
    gate_up(1, (-3, 3), False, False, 0, 6)
    pump(13)
    pwait(1, (6,))
    gate_up(1, (4,), False, True, 0, 6)
    pwait_own(2)

    def cc(o):
        return pl.ds(o * 128, 128)

    def pblk(o, c, mi, rws):
        return part.at[c, mi, :, rws, cc(o)] if o == 0 else part.at[c, :, mi, rws, cc(o)]

    def qblk(o, c, ni, rws):
        return part.at[c, x, ni, rws, cc(o)] if o == 0 else part.at[c, ni, y, rws, cc(o)]

    def link(step, c, o, di):
        m, n = major(o)
        d = DIRS[di]
        if step == 0:
            src, dst = pblk(o, c, w4(m + 2), half_rows(di)), r1.at[c, o, di]
        elif step == 1:
            src, dst = pblk(o, c, w4(m + d), every), r2.at[c, o, di]
        elif step == 2:
            src, dst = qblk(o, c, w4(n + 2), half_rows(di)), r3.at[c, o, di]
        else:
            src, dst = qblk(o, c, w4(n + d), every), r4.at[c, o, di]
        return remote(src, dst, qs.at[step, c, o, di], qr.at[step, c, o, di], nbr(o, step // 2, d))

    def both(fn):
        for o in range(2):
            for di in range(2):
                fn(o, di)

    def plus(ref, *more):
        total = ref[...].astype(F32)
        for v in more:
            total = total + v.astype(F32)
        ref[...] = total.astype(BF16)

    def origin(c):
        near = (c + 1) // 2
        return (z + NZ + jnp.where(c % 2 == 1, -near, near)) % NZ

    def chunk(c):
        zz = origin(c)
        for e in range(2):
            yv = jnp.dot(hid[e], wd[zz, e], preferred_element_type=F32).astype(BF16)
            ybuf[:, pl.ds(e * SLOTS, SLOTS), :] = yv.reshape(16, SLOTS, 256)

        def scatter(q):
            v = jnp.dot(pt[q], ybuf[q], preferred_element_type=F32).astype(BF16)
            sx, sy = source(q)
            part[c, sx, sy] = v

        across = [q for q in range(16) if 2 in SOURCES[q]]
        for q in across:
            scatter(q)
        both(lambda o, di: link(0, c, o, di).start())
        for q in range(16):
            if q not in across:
                scatter(q)

    def step2(c):
        def one(o, di):
            link(0, c, o, di).wait_recv()
            m = major(o)[0]
            plus(pblk(o, c, w4(m + DIRS[di]), half_rows(di)), r1[c, o, di])
            link(1, c, o, di).start()

        both(one)

    def step3(c):
        for o in range(2):
            for di in range(2):
                link(1, c, o, di).wait_recv()
            plus(pblk(o, c, major(o)[0], every), r2[c, o, 0], r2[c, o, 1])
            for di in range(2):
                link(2, c, o, di).start()

    def step4(c):
        def one(o, di):
            link(2, c, o, di).wait_recv()
            n = major(o)[1]
            plus(qblk(o, c, w4(n + DIRS[di]), half_rows(di)), r3[c, o, di])
            link(3, c, o, di).start()

        both(one)

    def result(c):
        cols = pl.ds(pl.multiple_of(origin(c) * 256, 256), 256)
        return pltpu.make_async_copy(outv.at[:, cols], out_ref.at[:, cols], osem.at[c])

    def step5(c):
        zz = origin(c)
        for o in range(2):
            for di in range(2):
                link(3, c, o, di).wait_recv()
            n = major(o)[1]
            total = qblk(o, c, n, every)[...].astype(F32) + r4[c, o, 0].astype(F32) + r4[c, o, 1].astype(F32)
            col = pl.multiple_of(zz * 256 + o * 128, 128)
            outv[:, pl.ds(col, 128)] = total.astype(BF16)
        result(c).start()
        for step in range(4):
            both(lambda o, di: link(step, c, o, di).wait_send())

    stages = ((0, chunk), (1, step2), (3, step3), (5, step4), (7, step5))

    def weights_in(c):
        if c == 1:
            pump(14)
        if c <= 5:
            pump(14 + c)
        if c < 7:
            hop = (c + 1) // 2
            pwait(2, (2 * hop - 2, 2 * hop - 1), ((c + 1) % 2,))
        if c == 6:
            pump(20)
        if c == 7:
            pwait(2, (6,))

    def turn(i, carry):
        for c in range(1, 8):
            @pl.when(i == c)
            def _(c=c):
                weights_in(c)
        for j, fn in stages:
            @pl.when((i >= j) & (i < NZ + j))
            def _(j=j, fn=fn):
                fn(i - j)

        @pl.when(i == 10)
        def _():
            for c in sends:
                c.wait_send()
            zdrain()

        return carry

    lax.fori_loop(0, NZ + stages[-1][0], turn, 0)

    def finish(c, carry):
        result(c).wait()
        return carry

    lax.fori_loop(0, NZ, finish, 0)


def layer(tokens, expert_ids, gate_weights, hot_ids, w_gate, w_up, w_down):
    dma = pltpu.SemaphoreType.DMA
    any_spec = pl.BlockSpec(memory_space=pl.ANY)
    return pl.pallas_call(
        kernel,
        out_shape=jax.ShapeDtypeStruct((128, 2048), BF16),
        in_specs=[any_spec] * 6,
        out_specs=any_spec,
        scratch_shapes=[
            pltpu.VMEM((4, 4, 128, 2048), BF16),
            pltpu.VMEM((4, 4, 8, 128), F32),
            pltpu.VMEM((4, 128), jnp.int32),
            pltpu.VMEM((4, 128), F32),
            pltpu.VMEM((2, 2048, 1536), BF16),
            pltpu.VMEM((8, 2, 768, 256), BF16),
            pltpu.VMEM((1024, 1536), F32),
            pltpu.VMEM((2, 1024, 768), BF16),
            pltpu.VMEM((2, 1024, 1), F32),
            pltpu.VMEM((16, 128, 128), BF16),
            pltpu.VMEM((16, 128, 256), BF16),
            pltpu.VMEM((8, 4, 4, 128, 256), BF16),
            pltpu.VMEM((8, 2, 2, 4, 64, 128), BF16),
            pltpu.VMEM((8, 2, 2, 4, 128, 128), BF16),
            pltpu.VMEM((8, 2, 2, 64, 128), BF16),
            pltpu.VMEM((8, 2, 2, 128, 128), BF16),
            pltpu.VMEM((128, 2048), BF16),
            dma((9,)),
            dma((2, 21)), dma((2, 21)),
            dma((3, 16)), dma((3, 16)),
            dma((4, 2, 2)), dma((4, 2, 2)),
            dma((6,)), dma((6,)),
            dma((4, 8, 2, 2)), dma((4, 8, 2, 2)),
            dma((8,)),
        ],
        compiler_params=pltpu.CompilerParams(
            collective_id=0, has_side_effects=True, vmem_limit_bytes=67043328
        ),
    )(tokens, expert_ids.T, gate_weights.T, w_gate, w_up, w_down)


def solution(mesh):
    placed = (
        P(("dp", "expert"), None),
        P(("dp", "expert"), None),
        P(("dp", "expert"), None),
        P(),
        P("expert", "dp", None),
        P("expert", "dp", None),
        P("expert", None, "dp"),
    )
    return jax.shard_map(
        layer, mesh=mesh, in_specs=placed, out_specs=P(("dp", "expert"), None), check_vma=False
    )
```

```python
import jax
import jax.numpy as jnp
from jax import lax
from jax.experimental import pallas as pl
from jax.experimental.pallas import tpu as pltpu
from jax.sharding import PartitionSpec as P

MESH = pl.DeviceIdType.MESH
NZ = 8
SIDE = 4
SLOTS = 64
DIRS = (1, -1)
NEAR = ((0, 0), (1, 0), (-1, 0), (0, 1), (0, -1), (1, 1), (1, -1), (-1, 1))
FAR = ((-1, -1), (2, 0), (2, 1), (2, -1), (0, 2), (1, 2), (-1, 2), (2, 2))
SOURCES = NEAR + FAR
F32 = jnp.float32
BF16 = jnp.bfloat16


def kernel(
    tok_in, ids_in, gw_in, wg_in, wu_in, wd_in, out_ref,
    tok, meta, ids, gw, wgu, wd, acc, hid, gs, pt, ybuf, part, r1, r2, r3, r4, outv,
    lsem, zs, zr, ps, pr, ts, tr, ms, mr, qs, qr, osem,
):
    dp = lax.axis_index("dp")
    ex = lax.axis_index("expert")
    z, k = dp // 2, dp % 2
    x, y = ex // SIDE, ex % SIDE

    def zdev(d):
        return (((z + d + NZ) % NZ) * 2 + k, ex)

    def xdev(d):
        return (dp, ((x + d + SIDE) % SIDE) * SIDE + y)

    def ydev(d):
        return (dp, x * SIDE + (y + d + SIDE) % SIDE)

    partner = (z * 2 + 1 - k, ex)

    def nbr(o, stage, d):
        return xdev(d) if (o + stage) % 2 == 0 else ydev(d)

    barrier = pltpu.get_barrier_semaphore()
    around = [zdev(1), zdev(-1), xdev(1), xdev(-1), ydev(1), ydev(-1), partner]
    for dev in around:
        pl.semaphore_signal(barrier, inc=1, device_id=dev, device_id_type=MESH)

    def zpiece(g, half, zz, core):
        if g < 2:
            rows = pl.multiple_of((zz * 2 + core) * 128, 128)
            return wgu.at[g, pl.ds(rows, 128), pl.ds(half * 768, 768)]
        cols = pl.multiple_of(core * 128, 128)
        return wd.at[zz, half, :, pl.ds(cols, 128)]

    local = []
    for g in range(2):
        for half, src in ((0, wg_in), (1, wu_in)):
            local.append((src.at[g], zpiece(g, half, z, k)))
    for half in range(2):
        local.append((wd_in.at[half], zpiece(2, half, z, k)))
    local.append((tok_in, tok.at[x, y]))
    local.append((ids_in, ids))
    local.append((gw_in, gw))
    local = [pltpu.make_async_copy(s, d, lsem.at[i]) for i, (s, d) in enumerate(local)]
    for c in local:
        c.start()
    for c in local[-2:]:
        c.wait()
    meta[x, y, pl.ds(0, 4)] = ids[...].astype(F32)
    meta[x, y, pl.ds(4, 4)] = gw[...]
    pl.semaphore_wait(barrier, len(around))
    for c in local[:-2]:
        c.wait()

    sends = []

    def remote(src, dst, ssem, rsem, dev):
        return pltpu.make_async_remote_copy(
            src_ref=src, dst_ref=dst, send_sem=ssem, recv_sem=rsem,
            device_id=dev, device_id_type=MESH,
        )

    def start(*a):
        c = remote(*a)
        c.start()
        sends.append(c)

    def arrival(di, r):
        return (r // 2 + 1, r % 2) if r < 6 else (4, di)

    def zdesc(g, half, hop, di):
        d = DIRS[di]
        piece = zpiece(g, half, (z - d * (hop - 1) + NZ) % NZ, k)
        n = g * 7 + ((hop - 1) * 2 + half if hop < 4 else 6)
        return remote(piece, piece, zs.at[di, n], zr.at[di, n], zdev(d))

    def pdesc(g, half, zz, i, core):
        piece = zpiece(g, half, zz, core)
        return remote(piece, piece, ps.at[g, i], pr.at[g, i], partner)

    def parrival(g, di, r, core):
        hop, half = arrival(di, r)
        return pdesc(g, half, (z - DIRS[di] * hop + NZ) % NZ, 2 + di * 7 + r, core)

    def own(g):
        for half in range(2):
            for di in range(2):
                zdesc(g, half, 1, di).start()
        for half in range(2):
            pdesc(g, half, z, half, k).start()

    def pump(n):
        g, r = n // 7, n % 7
        for di in range(2):
            d = DIRS[di]
            hop, half = arrival(di, r)
            piece = zpiece(g, half, (z - d * hop + NZ) % NZ, k)
            remote(piece, piece, zs.at[di, n], zr.at[di, n], zdev(d)).wait_recv()
            if hop < 3 or (hop == 3 and half == di):
                zdesc(g, half, hop + 1, di).start()
            parrival(g, di, r, k).start()
        if r == 5 and g < 2:
            own(g + 1)

    def pwait_own(g):
        for half in range(2):
            pdesc(g, half, z, half, 1 - k).wait_recv()

    def pwait(g, rs, dis=(0, 1)):
        for r in rs:
            for di in dis:
                parrival(g, di, r, 1 - k).wait_recv()

    def zdrain():
        for g in range(3):
            for half in range(2):
                pdesc(g, half, z, half, k).wait_send()
            for r in range(7):
                for di in range(2):
                    hop, half = arrival(di, r)
                    zdesc(g, half, hop, di).wait_send()
                    parrival(g, di, r, k).wait_send()

    def major(o):
        return (x, y) if o == 0 else (y, x)

    def half_rows(di):
        return pl.ds(di * 64, 64)

    every = pl.ds(0, 128)

    def tblk(o, mi, rows):
        n = major(o)[1]
        cols = pl.ds(o * 1024, 1024)
        return tok.at[mi, n, rows, cols] if o == 0 else tok.at[n, mi, rows, cols]

    def tcol(o, ni, rows):
        cols = pl.ds(o * 1024, 1024)
        return tok.at[:, ni, rows, cols] if o == 0 else tok.at[ni, :, rows, cols]

    def w4(v):
        return (v + SIDE) % SIDE

    def tok_step(step):
        for o in range(2):
            m, n = major(o)
            for di in range(2):
                d = DIRS[di]

                def got(s, ref):
                    remote(ref, ref, ts.at[s, o, di], tr.at[s, o, di], nbr(o, s // 2, d)).wait_recv()

                if step == 1:
                    got(0, tblk(o, w4(m - d), every))
                    ref = tblk(o, w4(m - d), half_rows(di))
                elif step == 2:
                    got(1, tblk(o, w4(m - 2 * d), half_rows(di)))
                elif step == 3:
                    got(2, tcol(o, w4(n - d), every))
                    ref = tcol(o, w4(n - d), half_rows(di))
                elif step == 4:
                    got(3, tcol(o, w4(n - 2 * d), half_rows(di)))
                if step in (1, 3):
                    start(ref, ref, ts.at[step, o, di], tr.at[step, o, di], nbr(o, step // 2, d))
            if step in (0, 2):
                ref = tblk(o, m, every) if step == 0 else tcol(o, n, every)
                for di in range(2):
                    start(ref, ref, ts.at[step, o, di], tr.at[step, o, di], nbr(o, step // 2, DIRS[di]))

    def meta_step(step):
        def go(i, ref, dev):
            start(ref, ref, ms.at[i], mr.at[i], dev)

        def got(i, ref, dev):
            remote(ref, ref, ms.at[i], mr.at[i], dev).wait_recv()

        if step == 0:
            go(0, meta.at[x, y], xdev(1))
            go(1, meta.at[x, y], xdev(-1))
        elif step == 1:
            got(0, meta.at[w4(x - 1), y], xdev(1))
            go(2, meta.at[w4(x - 1), y], xdev(1))
            got(1, meta.at[w4(x + 1), y], xdev(-1))
        elif step == 2:
            got(2, meta.at[w4(x - 2), y], xdev(1))
            go(3, meta.at[:, y], ydev(1))
            go(4, meta.at[:, y], ydev(-1))
        elif step == 3:
            got(3, meta.at[:, w4(y - 1)], ydev(1))
            go(5, meta.at[:, w4(y - 1)], ydev(1))
            got(4, meta.at[:, w4(y + 1)], ydev(-1))
        else:
            got(5, meta.at[:, w4(y - 2)], ydev(1))

    own(0)
    tok_step(0)
    meta_step(0)
    pump(0)
    meta_step(1)
    tok_step(1)
    pump(1)
    meta_step(2)
    tok_step(2)
    for n in range(2, 8):
        pump(n)
        if n == 3:
            meta_step(3)
        if n == 5:
            meta_step(4)
    tok_step(3)

    def source(q):
        return w4(x + SOURCES[q][0]), w4(y + SOURCES[q][1])

    rows = jnp.stack([meta[source(q)] for q in range(16)])
    mine = [(ex * 2).astype(F32), (ex * 2 + 1).astype(F32)]
    hits, gates = [], []
    for e in range(2):
        same = [rows[:, j, :] == mine[e] for j in range(4)]
        hits.append(sum(jnp.where(s, 1.0, 0.0) for s in same))
        gates.append(sum(jnp.where(s, rows[:, 4 + j, :], 0.0) for j, s in enumerate(same)))
    hit = jnp.concatenate(hits, axis=0)
    before = lax.broadcasted_iota(jnp.int32, (128, 128), 0) < lax.broadcasted_iota(jnp.int32, (128, 128), 1)
    rank = jnp.dot(hit.astype(BF16), jnp.where(before, 1.0, 0.0).astype(BF16), preferred_element_type=F32)
    lift = jnp.where(lax.broadcasted_iota(jnp.int32, (32, 128), 0) < 16, 0.0, float(SLOTS))
    slot = jnp.where(hit > 0.5, rank + lift, -1.0)
    slot_cols = jnp.transpose(jnp.concatenate([slot, jnp.zeros((96, 128), F32)], axis=0))

    down_i = lax.broadcasted_iota(jnp.int32, (128, 128), 0).astype(F32)
    across_i = lax.broadcasted_iota(jnp.int32, (128, 128), 1).astype(F32)

    def gather(qs_):
        for q in qs_:
            pick = (slot[q:q + 1] == down_i) | (slot[16 + q:17 + q] == down_i)
            gate_of = jnp.where(down_i < SLOTS, gates[0][q:q + 1], gates[1][q:q + 1])
            g_col = jnp.sum(jnp.where(pick, gate_of, 0.0), axis=1, keepdims=True)
            for e in range(2):
                gs[e, pl.ds(q * SLOTS, SLOTS), :] = g_col[e * SLOTS:(e + 1) * SLOTS]
            back = (slot_cols[:, q:q + 1] == across_i) | (slot_cols[:, 16 + q:17 + q] == across_i)
            pt[q] = jnp.where(back, 1.0, 0.0).astype(BF16)
            picked = jnp.where(pick, 1.0, 0.0).astype(BF16)
            got = jnp.dot(picked, tok[source(q)], preferred_element_type=F32).astype(BF16)
            for c in range(NZ):
                part[c, q // SIDE, q % SIDE] = got[:, c * 256:(c + 1) * 256]

    def gate_up(e, offs, first, last, lo, hi):
        def body(i, carry):
            mb = i // 3
            r0 = pl.multiple_of(mb * 512, 512)
            c0 = pl.multiple_of((i % 3) * 256, 256)
            c1 = pl.multiple_of(768 + (i % 3) * 256, 256)
            deep = range(NZ) if offs is None else [(z + off + NZ) % NZ for off in offs]
            rws = jnp.concatenate(
                [part[c, pl.ds(mb * 2, 2), :, pl.ds(e * SLOTS, SLOTS), :].reshape(512, 256) for c in deep], axis=1
            )
            sums = []
            for col in (c0, c1):
                w = jnp.concatenate(
                    [wgu[e, pl.ds(pl.multiple_of(c * 256, 256), 256), pl.ds(col, 256)] for c in deep], axis=0
                )
                total = jnp.dot(rws, w, preferred_element_type=F32)
                sums.append(total if first else total + acc[pl.ds(r0, 512), pl.ds(col, 256)])
            if last:
                gate, up = sums
                half = 0.5 * gate
                h = (half + half * jnp.tanh(half)) * up * gs[e, pl.ds(r0, 512), :]
                hid[e, pl.ds(r0, 512), pl.ds(c0, 256)] = h.astype(BF16)
            else:
                for col, total in zip((c0, c1), sums):
                    acc[pl.ds(r0, 512), pl.ds(col, 256)] = total
            return carry

        lax.fori_loop(lo, hi, body, 0)

    soon = (0, -1, 1, -2, 2)
    gather(range(8))
    pwait_own(0)
    pwait(0, range(7))
    gate_up(0, None, True, True, 0, 2)
    pump(8)
    gate_up(0, None, True, True, 2, 3)
    pump(9)
    tok_step(4)
    gather(range(8, 16))
    pump(10)
    gate_up(0, None, True, True, 3, 6)
    pump(11)
    pwait_own(1)
    pwait(1, range(4))
    gate_up(1, soon, True, False, 0, 4)
    pump(12)
    gate_up(1, soon, True, False, 4, 6)
    pwait(1, (4, 5))
    gate_up(1, (-3, 3), False, False, 0, 6)
    pump(13)
    pwait(1, (6,))
    gate_up(1, (4,), False, True, 0, 6)
    pwait_own(2)

    def cc(o):
        return pl.ds(o * 128, 128)

    def pblk(o, c, mi, rws):
        return part.at[c, mi, :, rws, cc(o)] if o == 0 else part.at[c, :, mi, rws, cc(o)]

    def qblk(o, c, ni, rws):
        return part.at[c, x, ni, rws, cc(o)] if o == 0 else part.at[c, ni, y, rws, cc(o)]

    def link(step, c, o, di):
        m, n = major(o)
        d = DIRS[di]
        if step == 0:
            src, dst = pblk(o, c, w4(m + 2), half_rows(di)), r1.at[c, o, di]
        elif step == 1:
            src, dst = pblk(o, c, w4(m + d), every), r2.at[c, o, di]
        elif step == 2:
            src, dst = qblk(o, c, w4(n + 2), half_rows(di)), r3.at[c, o, di]
        else:
            src, dst = qblk(o, c, w4(n + d), every), r4.at[c, o, di]
        return remote(src, dst, qs.at[step, c, o, di], qr.at[step, c, o, di], nbr(o, step // 2, d))

    def both(fn):
        for o in range(2):
            for di in range(2):
                fn(o, di)

    def plus(ref, *more):
        total = ref[...].astype(F32)
        for v in more:
            total = total + v.astype(F32)
        ref[...] = total.astype(BF16)

    def origin(c):
        near = (c + 1) // 2
        return (z + NZ + jnp.where(c % 2 == 1, -near, near)) % NZ

    def chunk(c):
        zz = origin(c)
        for e in range(2):
            yv = jnp.dot(hid[e], wd[zz, e], preferred_element_type=F32).astype(BF16)
            ybuf[:, pl.ds(e * SLOTS, SLOTS), :] = yv.reshape(16, SLOTS, 256)

        def scatter(q):
            v = jnp.dot(pt[q], ybuf[q], preferred_element_type=F32).astype(BF16)
            sx, sy = source(q)
            part[c, sx, sy] = v

        across = [q for q in range(16) if 2 in SOURCES[q]]
        for q in across:
            scatter(q)
        both(lambda o, di: link(0, c, o, di).start())
        for q in range(16):
            if q not in across:
                scatter(q)

    def step2(c):
        def one(o, di):
            link(0, c, o, di).wait_recv()
            m = major(o)[0]
            plus(pblk(o, c, w4(m + DIRS[di]), half_rows(di)), r1[c, o, di])
            link(1, c, o, di).start()

        both(one)

    def step3(c):
        for o in range(2):
            for di in range(2):
                link(1, c, o, di).wait_recv()
            plus(pblk(o, c, major(o)[0], every), r2[c, o, 0], r2[c, o, 1])
            for di in range(2):
                link(2, c, o, di).start()

    def step4(c):
        def one(o, di):
            link(2, c, o, di).wait_recv()
            n = major(o)[1]
            plus(qblk(o, c, w4(n + DIRS[di]), half_rows(di)), r3[c, o, di])
            link(3, c, o, di).start()

        both(one)

    def result(c):
        cols = pl.ds(pl.multiple_of(origin(c) * 256, 256), 256)
        return pltpu.make_async_copy(outv.at[:, cols], out_ref.at[:, cols], osem.at[c])

    def step5(c):
        zz = origin(c)
        for o in range(2):
            for di in range(2):
                link(3, c, o, di).wait_recv()
            n = major(o)[1]
            total = qblk(o, c, n, every)[...].astype(F32) + r4[c, o, 0].astype(F32) + r4[c, o, 1].astype(F32)
            col = pl.multiple_of(zz * 256 + o * 128, 128)
            outv[:, pl.ds(col, 128)] = total.astype(BF16)
        result(c).start()
        for step in range(4):
            both(lambda o, di: link(step, c, o, di).wait_send())

    stages = ((0, chunk), (1, step2), (3, step3), (5, step4), (7, step5))

    def weights_in(c):
        if c == 1:
            pump(14)
        if c <= 5:
            pump(14 + c)
        if c < 7:
            hop = (c + 1) // 2
            pwait(2, (2 * hop - 2, 2 * hop - 1), ((c + 1) % 2,))
        if c == 6:
            pump(20)
        if c == 7:
            pwait(2, (6,))

    def turn(i, carry):
        for c in range(1, 8):
            @pl.when(i == c)
            def _(c=c):
                weights_in(c)
        for j, fn in stages:
            @pl.when((i >= j) & (i < NZ + j))
            def _(j=j, fn=fn):
                fn(i - j)

        @pl.when(i == 10)
        def _():
            for c in sends:
                c.wait_send()
            zdrain()

        return carry

    lax.fori_loop(0, NZ + stages[-1][0], turn, 0)

    def finish(c, carry):
        result(c).wait()
        return carry

    lax.fori_loop(0, NZ, finish, 0)


def layer(tokens, expert_ids, gate_weights, hot_ids, w_gate, w_up, w_down):
    dma = pltpu.SemaphoreType.DMA
    any_spec = pl.BlockSpec(memory_space=pl.ANY)
    return pl.pallas_call(
        kernel,
        out_shape=jax.ShapeDtypeStruct((128, 2048), BF16),
        in_specs=[any_spec] * 6,
        out_specs=any_spec,
        scratch_shapes=[
            pltpu.VMEM((4, 4, 128, 2048), BF16),
            pltpu.VMEM((4, 4, 8, 128), F32),
            pltpu.VMEM((4, 128), jnp.int32),
            pltpu.VMEM((4, 128), F32),
            pltpu.VMEM((2, 2048, 1536), BF16),
            pltpu.VMEM((8, 2, 768, 256), BF16),
            pltpu.VMEM((1024, 1536), F32),
            pltpu.VMEM((2, 1024, 768), BF16),
            pltpu.VMEM((2, 1024, 1), F32),
            pltpu.VMEM((16, 128, 128), BF16),
            pltpu.VMEM((16, 128, 256), BF16),
            pltpu.VMEM((8, 4, 4, 128, 256), BF16),
            pltpu.VMEM((8, 2, 2, 4, 64, 128), BF16),
            pltpu.VMEM((8, 2, 2, 4, 128, 128), BF16),
            pltpu.VMEM((8, 2, 2, 64, 128), BF16),
            pltpu.VMEM((8, 2, 2, 128, 128), BF16),
            pltpu.VMEM((128, 2048), BF16),
            dma((9,)),
            dma((2, 21)), dma((2, 21)),
            dma((3, 16)), dma((3, 16)),
            dma((4, 2, 2)), dma((4, 2, 2)),
            dma((6,)), dma((6,)),
            dma((4, 8, 2, 2)), dma((4, 8, 2, 2)),
            dma((8,)),
        ],
        compiler_params=pltpu.CompilerParams(
            collective_id=0, has_side_effects=True, vmem_limit_bytes=67043328
        ),
    )(tokens, expert_ids.T, gate_weights.T, w_gate, w_up, w_down)


def solution(mesh):
    placed = (
        P(("dp", "expert"), None),
        P(("dp", "expert"), None),
        P(("dp", "expert"), None),
        P(),
        P("expert", "dp", None),
        P("expert", "dp", None),
        P("expert", None, "dp"),
    )
    return jax.shard_map(
        layer, mesh=mesh, in_specs=placed, out_specs=P(("dp", "expert"), None), check_vma=False
    )
```
